32 devices in a mesh: grp: 2 (over y), vec: 4 (over z), wlk: 4 (over x, core).
Axes of the slice: x: 2, y: 2, z: 4, core: 2. Of those that a mesh axis runs over, the one named last changes fastest.
Arguments:
- cholesky: bfloat16 [48, 64, 512], P(('grp', 'vec')), parts along dimension 0
- orbitals: float32 [32, 64, 512], P(('grp', 'vec', 'wlk')), parts along dimension 0, may hold values from -6 to 6
- log_weights: float32 [32], P(('grp', 'vec', 'wlk')), parts along dimension 0, may hold values from -6 to 6
- parents: int32 [32], P(('grp', 'vec', 'wlk')), parts along dimension 0, may hold values from 0 to 3
- propagator: float32 [1024, 512], P('grp'), parts along dimension 0
Outputs:
- new_orbitals: float32 [32, 64, 512], P(('grp', 'vec', 'wlk')), parts along dimension 0
- new_log_weights: float32 [32], P(('grp', 'vec', 'wlk')), parts along dimension 0
The draws below stay inside these ranges and needn't reach their ends.
There are 2 independent parts, one for each index of `grp`. The reference program is written for one: setup_inputs(seed, part) draws one part's arguments, and reference() takes and returns one part's arrays. A program takes and returns all parts, laid end to end along the dimension named above; each array names one. Nothing has to cross between parts.
Inputs may be any that keep to these rules, and one draw needn't show every extreme that they name: parents[w] counts within the aligned block of 4 consecutive walkers that holds w.
All inputs are finite; a program needn't handle non-finite values.
Results may differ from the reference program's by a relative error of at most 0.02.
Values may be sent and summed in bfloat16 or wider, within the bound.
A program may use at most 64 MiB of HBM per device.

```python
import math
import jax
import jax.numpy as jnp
import numpy as np
from jax import lax

NORB = 512
NOCC = 64
NS_ITERS = 2
NCHOL = 24
POPULATION = 4
WALKERS = 16


def draw_cholesky(key, part):
    noise_key = jax.random.fold_in(key, 11)
    position = jnp.arange(NCHOL, dtype=jnp.float32) / max(NCHOL - 1, 1)
    samples = jax.random.normal(noise_key, (NCHOL, NOCC, NORB), jnp.float32)
    falloff = 3.0 ** (1.0 - position)
    return (samples * falloff[:, None, None] / math.sqrt(NORB)).astype(jnp.bfloat16)


def draw_orbitals(key, part):
    noise_key = jax.random.fold_in(key, 37)
    values = jnp.clip(jax.random.normal(noise_key, (WALKERS, NOCC, NORB), jnp.float32), -6.0, 6.0)
    return values.astype(jnp.float32)


def draw_propagator(key, part):
    noise_key = jax.random.fold_in(key, 23)
    samples = jax.random.normal(noise_key, (NORB, NORB), jnp.float32)
    return jnp.eye(NORB, dtype=jnp.float32) + 0.5 * samples / math.sqrt(NORB)


def set_ends(result, stream_key, least, top_value):
    place = [jax.random.randint(jax.random.fold_in(stream_key, axis), (), 0, length) for axis, length in enumerate(result.shape)]
    main_axis = result.shape.index(max(result.shape))
    beside = place[:main_axis] + [(place[main_axis] + 1) % result.shape[main_axis]] + place[main_axis + 1:]
    return result.at[tuple(place)].set(least).at[tuple(beside)].set(top_value)


def block_scale(own_key, extent, shards, smallest, top_value):
    level = 1.0
    for dim, parts in shards:
        steps = jax.random.uniform(jax.random.fold_in(jax.random.fold_in(own_key, 6), dim), (parts,), jnp.float32, smallest / len(shards), top_value / len(shards))
        level = level * jnp.repeat(jnp.exp(steps), extent[dim] // parts).reshape((-1,) + (1,) * (len(extent) - 1 - dim))
    return level


def cumulative_ranks(count, lean):
    weights = [(1 << 20) // math.isqrt(standing ** lean) + 1 for standing in range(1, count + 1)]
    deviation = 1 + sum(weights) // (1 << 30)
    return np.cumsum(np.array([max(1, weight // deviation) for weight in weights]))


def ranked(key, shape, number_of, slope):
    table = cumulative_ranks(number_of, slope)
    ticket = jax.random.randint(jax.random.fold_in(key, 1), shape, 0, int(table[number_of - 1]))
    rank = jnp.searchsorted(jnp.asarray(table, jnp.int32), ticket, side="right")
    return jax.random.permutation(jax.random.fold_in(key, 2), number_of)[rank].astype(jnp.int32)


def gaussian(stream_key, dims, scale, limit, cuts=(), held_as=jnp.bfloat16):
    loudness = block_scale(stream_key, dims, cuts, -0.22, 0.18) if cuts else 1.0
    result = jax.random.normal(stream_key, dims, jnp.float32) * scale * loudness
    return jnp.minimum(jnp.maximum(result, -limit), limit).astype(held_as)


def setup_inputs(seed: int = 0, part: int = 0) -> dict:
    key_list = jax.random.split(jax.random.key(seed), 6)
    part_splits = jax.random.split(jax.random.fold_in(key_list[5], part), 6)
    return {
        "cholesky": draw_cholesky(jax.random.fold_in(jax.random.fold_in(key_list[5], part), 71), part),
        "orbitals": draw_orbitals(jax.random.fold_in(jax.random.fold_in(key_list[5], part), 71), part),
        "log_weights": gaussian(part_splits[2], (WALKERS,), 1.0, 6.0, ((0, 16),), jnp.float32),
        "parents": set_ends(ranked(part_splits[3], (WALKERS,), POPULATION, 2), jax.random.fold_in(part_splits[3], 3), 0, POPULATION - 1).astype(jnp.int32),
        "propagator": draw_propagator(jax.random.fold_in(jax.random.fold_in(key_list[5], part), 71), part),
    }


gradient_step = 0.25
energy_step = 0.002
epsilon = 1e-06

def reference(cholesky, orbitals, log_weights, parents, propagator):
    norm_scale = 1.0 / math.sqrt(NCHOL)
    chol_flat = cholesky.astype(jnp.float32).reshape(NCHOL * NOCC, NORB)
    identity = jnp.eye(NOCC, dtype=jnp.float32)

    def per_walker(orbital_rows):
        rounded = orbital_rows.astype(jnp.bfloat16)
        rounded = lax.optimization_barrier(rounded)
        theta = rounded.astype(jnp.float32)
        product = jnp.dot(theta, chol_flat.T)
        product = lax.optimization_barrier(product.astype(jnp.bfloat16))
        blocks = product.astype(jnp.float32).reshape(NOCC, NCHOL, NOCC)
        traces = lax.optimization_barrier(jnp.sum(blocks * identity[:, None, :], axis=(0, 2)))
        swapped = jnp.transpose(blocks, (2, 1, 0))
        exchange_sum = lax.optimization_barrier(jnp.sum(blocks * swapped, axis=(0, 2)))
        energy = 0.5 * norm_scale * jnp.sum(traces * traces - exchange_sum)
        adjoint = norm_scale * (traces[None, :, None] * identity[:, None, :] - swapped)
        adjoint = lax.optimization_barrier(adjoint.astype(jnp.bfloat16))
        adjoint = adjoint.astype(jnp.float32).reshape(NOCC, NCHOL * NOCC)
        gradient = jnp.dot(adjoint, chol_flat)
        return (energy, gradient)
    energies, gradients = lax.map(per_walker, orbitals)
    stepped = orbitals - gradient_step * gradients
    shifted = log_weights - energy_step * energies
    walker_ids = jnp.arange(WALKERS, dtype=jnp.int32)
    source = walker_ids // POPULATION * POPULATION + parents.astype(jnp.int32)
    chosen = stepped[source]
    new_log_weights = shifted[source]
    propagated = jnp.einsum('wjq,pq->wjp', chosen, propagator, precision=lax.Precision.HIGHEST)
    mean_square = lax.optimization_barrier(jnp.mean(propagated * propagated, axis=(1, 2)))
    current = propagated / jnp.sqrt(mean_square + epsilon)[:, None, None]
    for repeat_index in range(NS_ITERS):
        intersection = jnp.einsum('wjp,wkp->wjk', current, current, precision=lax.Precision.HIGHEST) / NORB
        current = 0.5 * (3.0 * current - jnp.einsum('wjk,wkp->wjp', intersection, current, precision=lax.Precision.HIGHEST))
    return (current, new_log_weights)
```

```python
import functools
import math

import jax
import jax.numpy as jnp
from jax import lax
from jax.experimental import pallas as pl
from jax.experimental.pallas import tpu as pltpu
from jax.sharding import PartitionSpec as P

NS_ITERS = 2

gradient_step = 0.25
energy_step = 0.002
epsilon = 1e-06

MESH = pl.DeviceIdType.MESH
UNROLL_LIMIT = 8
PIECES = 3
EXTRA = 16


def dot(a, b):
    return lax.dot_general(a, b, (((1,), (0,)), ((), ())), preferred_element_type=jnp.float32)


def dot_t(a, b):
    return lax.dot_general(a, b, (((1,), (1,)), ((), ())), preferred_element_type=jnp.float32)


def each(count, body):
    if count <= UNROLL_LIMIT:
        for j in range(count):
            body(j)
    else:
        lax.fori_loop(0, count, lambda j, c: (body(j), c)[1], 0)


def kernel(
    n_vec, n_wlk, vecs, pieces,
    chol_hbm, orb_hbm, logw, par, prop_hbm,
    out_ref, outlog_ref,
    orb, prop, propb, pop, turned, shared, acc,
    load_sem, own_sem, recv, d_send, u_send, r_send, x_send, s_send, p_recv, px_send, ps_send,
    up_ready, x_ready, sib_ready,
):
    me = lax.axis_index("vec")
    mw = lax.axis_index("wlk")
    occ, basis = orb.shape
    rows = vecs * occ
    share = rows // n_wlk
    step = share // pieces
    n_chip = n_wlk // 2
    chip, core = lax.div(mw, 2), lax.rem(mw, 2)
    sibling = mw + 1 - 2 * core
    others = n_vec - 1
    scale = 1.0 / math.sqrt(vecs * n_vec)

    def remote(src_ref, dst_ref, send, recv, where):
        return pltpu.make_async_remote_copy(
            src_ref=src_ref, dst_ref=dst_ref, send_sem=send, recv_sem=recv,
            device_id=where, device_id_type=MESH)

    def at(w, k):
        return pl.ds(pl.multiple_of(w * share + k * step, step), step)

    def quarter(w):
        return pl.ds(pl.multiple_of(w * share, share), share)

    def peer(j):
        return lax.rem(chip + 1 + j, n_chip) * 2 + core

    def down(dst, k):
        return remote(chol_hbm.at[at(mw, k)], shared.at[me, at(mw, k)],
                      d_send.at[dst], recv.at[me, mw, k], {"vec": dst})

    def up_own(k):
        return remote(chol_hbm.at[at(mw, k)], shared.at[me, at(mw, k)],
                      u_send.at[me], recv.at[me, mw, k], {"vec": me + 1})

    def up_relay(src, k):
        return remote(shared.at[src, at(mw, k)], shared.at[src, at(mw, k)],
                      u_send.at[src], recv.at[src, mw, k], {"vec": me + 1})

    def down_relay(k):
        return remote(shared.at[2, at(mw, k)], shared.at[2, at(mw, k)],
                      r_send, recv.at[2, mw, k], {"vec": 0})

    def across(src, w, k):
        return remote(shared.at[src, at(mw, k)], shared.at[src, at(mw, k)],
                      x_send.at[src, w], recv.at[src, mw, k], {"wlk": w})

    def beside(src, w, k):
        return remote(shared.at[src, at(w, k)], shared.at[src, at(w, k)],
                      s_send.at[src, w], recv.at[src, w, k], {"wlk": sibling})

    def arrived(src, w, k):
        remote(shared.at[src, at(w, k)], shared.at[src, at(w, k)],
               s_send.at[src, w], recv.at[src, w, k], {"wlk": sibling}).wait_recv()

    def walker_across(w):
        return remote(pop.at[mw], pop.at[mw], px_send.at[w], p_recv.at[mw], {"wlk": w})

    def walker_beside(w):
        return remote(pop.at[w], pop.at[w], ps_send.at[w], p_recv.at[w], {"wlk": sibling})

    def own_copy():
        return pltpu.make_async_copy(chol_hbm, shared.at[me], own_sem)

    load_orb = pltpu.make_async_copy(orb_hbm, orb, load_sem.at[0])
    load_prop = pltpu.make_async_copy(prop_hbm, prop, load_sem.at[1])

    barrier = pltpu.get_barrier_semaphore()
    for i in range(1, n_vec):
        @pl.when(i > me)
        def _():
            pl.semaphore_signal(barrier, inc=1, device_id={"vec": i}, device_id_type=MESH)
    for i in range(1, n_chip):
        @pl.when(i > chip)
        def _():
            pl.semaphore_signal(barrier, inc=1, device_id={"wlk": i * 2 + core}, device_id_type=MESH)

    @pl.when(core == 0)
    def _():
        pl.semaphore_signal(barrier, inc=1, device_id={"wlk": sibling}, device_id_type=MESH)

    load_orb.start()
    own_copy().start()
    load_prop.start()
    before = me + chip + core

    @pl.when(before > 0)
    def _():
        pl.semaphore_wait(barrier, before)

    relayed = n_vec >= 3

    def goes_down(d):
        return (d < me) & ((d != 0) | (me != 2)) if relayed else d < me

    for d in range(n_vec - 1):
        @pl.when(goes_down(d))
        def _():
            for k in range(pieces):
                down(d, k).start()

    @pl.when(me > 0)
    def _():
        pl.semaphore_signal(up_ready, inc=1, device_id={"vec": me - 1}, device_id_type=MESH)
    for i in range(n_chip - 1):
        @pl.when(i < chip)
        def _():
            pl.semaphore_signal(
                x_ready.at[chip], inc=1, device_id={"wlk": i * 2 + core}, device_id_type=MESH)

    @pl.when(core == 1)
    def _():
        pl.semaphore_signal(sib_ready, inc=1, device_id={"wlk": sibling}, device_id_type=MESH)

    load_orb.wait()
    pop[mw, 0:occ] = orb[...].astype(jnp.bfloat16)
    whole = jnp.full((EXTRA, basis), logw[0], jnp.float32)
    high = whole.astype(jnp.bfloat16)
    rest = whole - high.astype(jnp.float32)
    middle = rest.astype(jnp.bfloat16)
    low = (rest - middle.astype(jnp.float32)).astype(jnp.bfloat16)
    lane = lax.broadcasted_iota(jnp.int32, (EXTRA, basis), 1)
    pop[mw, occ:occ + EXTRA] = jnp.where(
        lane == 0, high.astype(jnp.float32),
        jnp.where(lane == 1, middle.astype(jnp.float32),
                  jnp.where(lane == 2, low.astype(jnp.float32), 0.0))).astype(jnp.bfloat16)
    for i in range(1, n_chip):
        @pl.when(i > chip)
        def _():
            pl.semaphore_wait(x_ready.at[i], 1)
    for j in range(n_chip - 1):
        walker_across(peer(j)).start()

    @pl.when(core == 0)
    def _():
        pl.semaphore_wait(sib_ready, 1)
    walker_beside(mw).start()

    @pl.when(me < n_vec - 1)
    def _():
        pl.semaphore_wait(up_ready, 1)
        for k in range(pieces):
            up_own(k).start()

    load_prop.wait()
    propb[...] = prop[...].T.astype(jnp.bfloat16)

    def source(j):
        lower = me - 1 - j
        return jnp.where(lower >= 0, lower, j + 1) if isinstance(j, int) else lax.select(
            lower >= 0, lower, j + 1)

    def take(j, k):
        src = source(j)
        arrived(src, mw, k)
        for i in range(n_chip - 1):
            across(src, peer(i), k).start()
        beside(src, mw, k).start()

        @pl.when((src < me) & (me < n_vec - 1))
        def _():
            up_relay(src, k).start()
        if relayed:
            @pl.when((src == 2) & (me == 1))
            def _():
                down_relay(k).start()

    def pass_on(j, k):
        src = source(j)
        for i in range(n_chip - 1):
            arrived(src, peer(i), k)
            beside(src, peer(i), k).start()

    for j in range(n_chip - 1):
        remote(pop.at[peer(j)], pop.at[peer(j)], ps_send.at[peer(j)], p_recv.at[peer(j)],
               {"wlk": sibling}).wait_recv()
        walker_beside(peer(j)).start()
    for j in range(n_chip):
        other = lax.rem(chip + j, n_chip) * 2 + 1 - core
        remote(pop.at[other], pop.at[other], ps_send.at[other], p_recv.at[other],
               {"wlk": sibling}).wait_recv()
    parent = par[0]
    rows_of = jnp.full((occ + EXTRA, basis), parent, jnp.int32)
    picked = pop[0].astype(jnp.float32)
    for m in range(1, n_wlk):
        picked = jnp.where(rows_of == m, pop[m].astype(jnp.float32), picked)
    theta = picked[0:occ]
    extra = picked[occ:occ + 8, 0:128]
    chosen_log = jnp.sum(extra, axis=1, keepdims=True)
    turned[...] = theta.T.astype(jnp.bfloat16)
    acc[...] = jnp.zeros_like(acc)

    row = lax.broadcasted_iota(jnp.int32, (occ, occ), 0)
    col = lax.broadcasted_iota(jnp.int32, (occ, occ), 1)
    diagonal = row == col

    def work(src, first, count):
        vectors = shared[src, first * occ:(first + count) * occ] if isinstance(first, int) else shared[
            src, pl.ds(pl.multiple_of(first * occ, occ), count * occ)]
        s = dot(vectors, turned[...])
        blocks = []
        for g in range(count):
            sg = s[g * occ:(g + 1) * occ, :]
            on_diagonal = jnp.where(diagonal, sg, 0.0)
            tg = jnp.sum(jnp.sum(on_diagonal, axis=0, keepdims=True), axis=1, keepdims=True)
            blocks.append((scale * (jnp.where(diagonal, tg, 0.0) - sg)).astype(jnp.bfloat16))
        adjoint = jnp.concatenate(blocks, axis=1) if count > 1 else blocks[0]
        acc[...] += dot(adjoint, vectors)

    own_copy().wait()
    work(me, 0, vecs)

    near = n_chip == 2 and vecs % 2 == 0
    half = vecs // 2

    def near_part(j):
        src = source(j)
        for k in range(pieces):
            arrived(src, sibling, k)
        work(src, chip * half, half)

    def far_part(j):
        src = source(j)
        for k in range(pieces):
            arrived(src, (1 - chip) * 2 + 1 - core, k)
        work(src, (1 - chip) * half, half)

    def all_parts(j):
        src = source(j)
        for i in range(n_chip):
            for k in range(pieces):
                arrived(src, lax.rem(chip + i, n_chip) * 2 + 1 - core, k)
        work(src, 0, vecs)

    if near and others <= UNROLL_LIMIT:
        for j in range(others + 2):
            for k in range(pieces):
                if j < others:
                    take(j, k)
                if 1 <= j <= others:
                    pass_on(j - 1, k)
            if 1 <= j <= others:
                near_part(j - 1)
            if j >= 2:
                far_part(j - 2)
    else:
        def one(j):
            for k in range(pieces):
                take(j, k)
            for k in range(pieces):
                pass_on(j, k)
            all_parts(j)

        each(others, one)

    gradient = acc[...]
    energy = 0.5 * jnp.sum(jnp.sum(theta * gradient, axis=0, keepdims=True), axis=1, keepdims=True)
    outlog_ref[...] = jnp.broadcast_to(chosen_log - energy_step * energy, (8, 128))
    stepped = theta - gradient_step * gradient
    x = dot(stepped.astype(jnp.bfloat16), propb[...])
    mean_square = jnp.sum(jnp.sum(x * x, axis=0, keepdims=True), axis=1, keepdims=True)
    mean_square = mean_square / (occ * basis)
    norm = 1.0 / jnp.sqrt(mean_square + epsilon)
    for it in range(NS_ITERS):
        xb = x.astype(jnp.bfloat16)
        inter = dot_t(xb, xb) * (norm * norm / basis if it == 0 else 1.0 / basis)
        x = 0.5 * (3.0 * x - dot(inter.astype(jnp.bfloat16), xb))
        if it == 0:
            x = norm * x
    out_ref[...] = x

    def sent(send):
        remote(shared.at[0, quarter(0)], shared.at[0, quarter(0)], send, recv.at[0, 0, 0],
               {"wlk": sibling}).wait_send()

    for d in range(n_vec - 1):
        pl.when(goes_down(d))(lambda: sent(d_send.at[d]))

    @pl.when(me < n_vec - 1)
    def _():
        sent(u_send.at[me])

    def drain(j):
        src = source(j)
        pl.when((src < me) & (me < n_vec - 1))(lambda: sent(u_send.at[src]))
        for i in range(n_chip - 1):
            sent(x_send.at[src, peer(i)])
        for i in range(n_chip):
            sent(s_send.at[src, lax.rem(chip + i, n_chip) * 2 + core])

    each(others, drain)
    if relayed:
        pl.when(me == 1)(lambda: sent(r_send))
    for j in range(n_chip - 1):
        walker_across(peer(j)).wait_send()
    for j in range(n_chip):
        walker_beside(lax.rem(chip + j, n_chip) * 2 + core).wait_send()


def deliver(x_ref, log_ref, out_ref, outlog_ref, sem):
    copies = [
        pltpu.make_async_copy(log_ref.at[0:1], outlog_ref, sem.at[0]),
        pltpu.make_async_copy(x_ref, out_ref, sem.at[1]),
    ]
    for copy in copies:
        copy.start()
    for copy in copies:
        copy.wait()


def solution(mesh):
    n_vec, n_wlk = mesh.shape["vec"], mesh.shape["wlk"]

    def local(cholesky, orbitals, log_weights, parents, propagator):
        walkers, occ, basis = orbitals.shape
        assert walkers == 1 and n_wlk % 2 == 0
        vecs = cholesky.shape[0]
        share = vecs * occ // n_wlk
        assert share * n_wlk == vecs * occ
        pieces = PIECES if n_vec <= UNROLL_LIMIT and share % (16 * PIECES) == 0 else 1
        f32, bf16 = jnp.float32, jnp.bfloat16
        dma = pltpu.SemaphoreType.DMA
        regular = pltpu.SemaphoreType.REGULAR
        hbm = pl.BlockSpec(memory_space=pltpu.HBM)
        smem = pl.BlockSpec(memory_space=pltpu.SMEM)
        vmem = pl.BlockSpec(memory_space=pltpu.VMEM)
        x, logs = pl.pallas_call(
            functools.partial(kernel, n_vec, n_wlk, vecs, pieces),
            out_shape=(pltpu.VMEM((occ, basis), f32), pltpu.VMEM((8, 128), f32)),
            in_specs=[hbm, hbm, smem, smem, hbm],
            out_specs=(vmem, vmem),
            scratch_shapes=[
                pltpu.VMEM((occ, basis), f32),
                pltpu.VMEM(propagator.shape, f32),
                pltpu.VMEM(propagator.shape, bf16),
                pltpu.VMEM((n_wlk, occ + EXTRA, basis), bf16),
                pltpu.VMEM((basis, occ), bf16),
                pltpu.VMEM((n_vec, vecs * occ, basis), bf16),
                pltpu.VMEM((occ, basis), f32),
                dma((2,)), dma, dma((n_vec, n_wlk, pieces)),
                dma((n_vec,)), dma((n_vec,)), dma, dma((n_vec, n_wlk)), dma((n_vec, n_wlk)),
                dma((n_wlk,)), dma((n_wlk,)), dma((n_wlk,)),
                regular, regular((n_wlk // 2,)), regular,
            ],
            compiler_params=pltpu.CompilerParams(
                collective_id=0, has_side_effects=True, vmem_limit_bytes=60000000),
        )(
            cholesky.reshape(vecs * occ, basis),
            orbitals.reshape(occ, basis),
            log_weights,
            parents,
            propagator,
        )

        def here(array):
            return pltpu.with_memory_space_constraint(array, pltpu.VMEM)

        out, log = pl.pallas_call(
            deliver,
            out_shape=(
                jax.ShapeDtypeStruct((occ, basis), f32),
                jax.ShapeDtypeStruct((1, 128), f32),
            ),
            in_specs=[vmem, vmem],
            out_specs=(hbm, hbm),
            scratch_shapes=[dma((2,))],
        )(here(x), here(logs))
        return out.reshape(orbitals.shape), log[0, :1]

    placed = (
        P(("grp", "vec"), None, None),
        P(("grp", "vec", "wlk"), None, None),
        P(("grp", "vec", "wlk")),
        P(("grp", "vec", "wlk")),
        P("grp", None),
    )
    return jax.shard_map(
        local,
        mesh=mesh,
        in_specs=placed,
        out_specs=(P(("grp", "vec", "wlk"), None, None), P(("grp", "vec", "wlk"))),
        check_vma=False,
    )
```

```python
import functools
import math

import jax
import jax.numpy as jnp
from jax import lax
from jax.experimental import pallas as pl
from jax.experimental.pallas import tpu as pltpu
from jax.sharding import PartitionSpec as P

NS_ITERS = 2

gradient_step = 0.25
energy_step = 0.002
epsilon = 1e-06

MESH = pl.DeviceIdType.MESH
UNROLL_LIMIT = 8
PIECES = 3
EXTRA = 16


def dot(a, b):
    return lax.dot_general(a, b, (((1,), (0,)), ((), ())), preferred_element_type=jnp.float32)


def dot_t(a, b):
    return lax.dot_general(a, b, (((1,), (1,)), ((), ())), preferred_element_type=jnp.float32)


def each(count, body):
    if count <= UNROLL_LIMIT:
        for j in range(count):
            body(j)
    else:
        lax.fori_loop(0, count, lambda j, c: (body(j), c)[1], 0)


def kernel(
    n_vec, n_wlk, vecs, pieces,
    chol_hbm, orb_hbm, logw, par, prop_hbm,
    out_ref, outlog_ref,
    orb, prop, propb, pop, turned, shared, acc,
    load_sem, z_recv, x_recv, near_recv, far_recv, p_recv, v_send, p_send,
    z_ready, x_ready, sib_ready,
):
    me = lax.axis_index("vec")
    mw = lax.axis_index("wlk")
    occ, basis = orb.shape
    rows = vecs * occ
    share = rows // n_wlk
    step = share // pieces
    n_chip = n_wlk // 2
    chip, core = lax.div(mw, 2), lax.rem(mw, 2)
    sibling = mw + 1 - 2 * core
    others, chips = n_vec - 1, n_chip - 1
    scale = 1.0 / math.sqrt(vecs * n_vec)

    def remote(src_ref, dst_ref, send, recv, where):
        return pltpu.make_async_remote_copy(
            src_ref=src_ref, dst_ref=dst_ref, send_sem=send, recv_sem=recv,
            device_id=where, device_id_type=MESH)

    def at(w, k):
        return pl.ds(pl.multiple_of(w * share + k * step, step), step)

    def quarter(w):
        return pl.ds(pl.multiple_of(w * share, share), share)

    def slot(src, dst):
        return jnp.where(src > dst, src - 1, src)

    def peer(i):
        return lax.rem(chip + 1 + i, n_chip) * 2 + core

    def source(j):
        lower = me - 1 - j
        return jnp.where(lower >= 0, lower, j + 1)

    def along(dst, k):
        return remote(chol_hbm.at[at(mw, k)], shared.at[me, at(mw, k)],
                      v_send, z_recv.at[slot(me, dst), k], {"vec": dst})

    def from_along(src, k):
        remote(shared.at[src, at(mw, k)], shared.at[src, at(mw, k)],
               v_send, z_recv.at[slot(src, me), k], {"wlk": sibling}).wait_recv()

    def across(src, i, k):
        return remote(shared.at[src, at(mw, k)], shared.at[src, at(mw, k)],
                      v_send, x_recv.at[slot(src, me), chips - 1 - i, k], {"wlk": peer(i)})

    def from_across(src, i, k):
        remote(shared.at[src, at(peer(i), k)], shared.at[src, at(peer(i), k)],
               v_send, x_recv.at[slot(src, me), i, k], {"wlk": sibling}).wait_recv()

    def beside(src, k):
        return remote(shared.at[src, at(mw, k)], shared.at[src, at(mw, k)],
                      v_send, near_recv.at[slot(src, me)], {"wlk": sibling})

    def from_beside(src):
        remote(shared.at[src, quarter(sibling)], shared.at[src, quarter(sibling)],
               v_send, near_recv.at[slot(src, me)], {"wlk": sibling}).wait_recv()

    def beyond(src, i, k):
        return remote(shared.at[src, at(peer(i), k)], shared.at[src, at(peer(i), k)],
                      v_send, far_recv.at[slot(src, me), i], {"wlk": sibling})

    def from_beyond(src, i):
        w = peer(i) + 1 - 2 * core
        remote(shared.at[src, quarter(w)], shared.at[src, quarter(w)],
               v_send, far_recv.at[slot(src, me), i], {"wlk": sibling}).wait_recv()

    def walker(w, index, where):
        return remote(pop.at[w], pop.at[w], p_send, p_recv.at[index], {"wlk": where})

    load_orb = pltpu.make_async_copy(orb_hbm, orb, load_sem.at[0])
    load_own = pltpu.make_async_copy(chol_hbm, shared.at[me], load_sem.at[1])
    load_prop = pltpu.make_async_copy(prop_hbm, prop, load_sem.at[2])

    barrier = pltpu.get_barrier_semaphore()

    def greet(semaphore, where):
        pl.semaphore_signal(semaphore, inc=1, device_id=where, device_id_type=MESH)

    each(others, lambda j: pl.when(j + 1 > me)(lambda: greet(barrier, {"vec": j + 1})))
    each(chips, lambda j: pl.when(j + 1 > chip)(
        lambda: greet(barrier, {"wlk": (j + 1) * 2 + core})))
    pl.when(core == 0)(lambda: greet(barrier, {"wlk": sibling}))

    load_orb.start()
    before = me + chip + core
    pl.when(before > 0)(lambda: pl.semaphore_wait(barrier, before))

    each(others, lambda j: pl.when(j < me)(lambda: greet(z_ready.at[me - 1], {"vec": j})))
    each(chips, lambda j: pl.when(j < chip)(
        lambda: greet(x_ready.at[chip - 1], {"wlk": j * 2 + core})))
    pl.when(core == 1)(lambda: greet(sib_ready, {"wlk": sibling}))

    def send_along(dst):
        for k in range(pieces):
            along(dst, k).start()

    each(others, lambda j: pl.when(j < me)(lambda: send_along(j)))
    load_own.start()
    load_prop.start()

    load_orb.wait()
    pop[mw, 0:occ] = orb[...].astype(jnp.bfloat16)
    whole = jnp.full((EXTRA, basis), logw[0], jnp.float32)
    high = whole.astype(jnp.bfloat16).astype(jnp.float32)
    middle = (whole - high).astype(jnp.bfloat16).astype(jnp.float32)
    low = whole - high - middle
    lane = lax.broadcasted_iota(jnp.int32, (EXTRA, basis), 1)
    pop[mw, occ:occ + EXTRA] = jnp.where(
        lane == 0, high,
        jnp.where(lane == 1, middle, jnp.where(lane == 2, low, 0.0))).astype(jnp.bfloat16)

    pl.when(core == 0)(lambda: pl.semaphore_wait(sib_ready, 1))
    walker(mw, 2 * chips, sibling).start()
    each(chips, lambda j: pl.when(j + 1 > chip)(lambda: pl.semaphore_wait(x_ready.at[j], 1)))
    for i in range(chips):
        walker(mw, chips - 1 - i, peer(i)).start()

    def send_up(j):
        @pl.when(me + j + 1 < n_vec)
        def _():
            pl.semaphore_wait(z_ready.at[me + j], 1)
            send_along(me + j + 1)

    def take(j, k):
        src = source(j)
        from_along(src, k)
        for i in range(chips):
            across(src, i, k).start()
        beside(src, k).start()

    def pass_on(j, k):
        src = source(j)
        for i in range(chips):
            from_across(src, i, k)
            beyond(src, i, k).start()

    def pass_walkers():
        for i in range(chips):
            walker(peer(i), i, sibling).wait_recv()
            walker(peer(i), chips + i, sibling).start()

    def all_walkers():
        for i in range(chips + 1):
            w = peer(i) + 1 - 2 * core
            walker(w, chips + i, sibling).wait_recv()

    row = lax.broadcasted_iota(jnp.int32, (occ, occ), 0)
    col = lax.broadcasted_iota(jnp.int32, (occ, occ), 1)
    diagonal = row == col

    def work(src, first, count):
        vectors = shared[src, pl.ds(pl.multiple_of(first * occ, occ), count * occ)]
        s = dot(vectors, turned[...])
        blocks = []
        for g in range(count):
            sg = s[g * occ:(g + 1) * occ, :]
            on_diagonal = jnp.where(diagonal, sg, 0.0)
            tg = jnp.sum(jnp.sum(on_diagonal, axis=0, keepdims=True), axis=1, keepdims=True)
            blocks.append((scale * (jnp.where(diagonal, tg, 0.0) - sg)).astype(jnp.bfloat16))
        adjoint = jnp.concatenate(blocks, axis=1) if count > 1 else blocks[0]
        acc[...] += dot(adjoint, vectors)

    def choose():
        rows_of = jnp.full((occ + EXTRA, basis), par[0], jnp.int32)
        picked = pop[0].astype(jnp.float32)
        for m in range(1, n_wlk):
            picked = jnp.where(rows_of == m, pop[m].astype(jnp.float32), picked)
        turned[...] = picked[0:occ].T.astype(jnp.bfloat16)
        orb[...] = picked[0:occ]
        outlog_ref[...] = jnp.broadcast_to(
            jnp.sum(picked[occ:occ + 8, 0:128], axis=1, keepdims=True), (8, 128))
        acc[...] = jnp.zeros_like(acc)

    def turn_propagator():
        load_prop.wait()
        propb[...] = prop[...].T.astype(jnp.bfloat16)

    half = vecs // 2

    def near_part(j):
        from_beside(source(j))
        work(source(j), chip * half, half)

    def far_part(j):
        from_beyond(source(j), 0)
        work(source(j), (1 - chip) * half, half)

    if n_chip == 2 and vecs % 2 == 0 and 2 <= others <= UNROLL_LIMIT:
        send_up(0)
        for k in range(pieces):
            take(0, k)
        send_up(1)
        pass_walkers()
        turn_propagator()
        all_walkers()
        choose()
        load_own.wait()
        work(me, 0, half)
        for j in range(2, others):
            send_up(j)
        for j in range(1, others + 2):
            for k in range(pieces):
                if j < others:
                    take(j, k)
                if j <= others:
                    pass_on(j - 1, k)
                if k == 0:
                    if j == 1:
                        work(me, half, half)
                    else:
                        far_part(j - 2)
            if j <= others:
                near_part(j - 1)
    else:
        each(others, send_up)
        pass_walkers()
        turn_propagator()
        all_walkers()
        choose()
        load_own.wait()
        work(me, 0, vecs)

        def one(j):
            for k in range(pieces):
                take(j, k)
            for k in range(pieces):
                pass_on(j, k)
            from_beside(source(j))
            for i in range(chips):
                from_beyond(source(j), i)
            work(source(j), 0, vecs)

        each(others, one)

    theta = orb[...]
    gradient = acc[...]
    energy = 0.5 * jnp.sum(jnp.sum(theta * gradient, axis=0, keepdims=True), axis=1, keepdims=True)
    outlog_ref[...] -= energy_step * jnp.broadcast_to(energy, (8, 128))
    stepped = theta - gradient_step * gradient
    x = dot(stepped.astype(jnp.bfloat16), propb[...])
    mean_square = jnp.sum(jnp.sum(x * x, axis=0, keepdims=True), axis=1, keepdims=True)
    mean_square = mean_square / (occ * basis)
    norm = 1.0 / jnp.sqrt(mean_square + epsilon)
    for it in range(NS_ITERS):
        xb = x.astype(jnp.bfloat16)
        inter = dot_t(xb, xb) * (norm * norm / basis if it == 0 else 1.0 / basis)
        x = 0.5 * (3.0 * x - dot(inter.astype(jnp.bfloat16), xb))
        if it == 0:
            x = norm * x
    out_ref[...] = x

    every = shared.at[pl.ds(0, others)]
    remote(every, every, v_send, v_send, {"wlk": sibling}).wait_send()
    walkers = pop.at[pl.ds(0, n_wlk - 1)]
    remote(walkers, walkers, p_send, p_send, {"wlk": sibling}).wait_send()


def deliver(x_ref, log_ref, out_ref, outlog_ref, sem):
    copies = [
        pltpu.make_async_copy(log_ref.at[0:1], outlog_ref, sem.at[0]),
        pltpu.make_async_copy(x_ref, out_ref, sem.at[1]),
    ]
    for copy in copies:
        copy.start()
    for copy in copies:
        copy.wait()


def solution(mesh):
    n_vec, n_wlk = mesh.shape["vec"], mesh.shape["wlk"]

    def local(cholesky, orbitals, log_weights, parents, propagator):
        walkers, occ, basis = orbitals.shape
        assert walkers == 1 and n_wlk % 2 == 0
        vecs = cholesky.shape[0]
        share = vecs * occ // n_wlk
        assert share * n_wlk == vecs * occ
        pieces = PIECES if n_vec <= UNROLL_LIMIT and share % (16 * PIECES) == 0 else 1
        others, chips = n_vec - 1, n_wlk // 2 - 1
        f32, bf16 = jnp.float32, jnp.bfloat16
        dma = pltpu.SemaphoreType.DMA
        regular = pltpu.SemaphoreType.REGULAR
        hbm = pl.BlockSpec(memory_space=pltpu.HBM)
        smem = pl.BlockSpec(memory_space=pltpu.SMEM)
        vmem = pl.BlockSpec(memory_space=pltpu.VMEM)
        x, logs = pl.pallas_call(
            functools.partial(kernel, n_vec, n_wlk, vecs, pieces),
            out_shape=(pltpu.VMEM((occ, basis), f32), pltpu.VMEM((8, 128), f32)),
            in_specs=[hbm, hbm, smem, smem, hbm],
            out_specs=(vmem, vmem),
            scratch_shapes=[
                pltpu.VMEM((occ, basis), f32),
                pltpu.VMEM(propagator.shape, f32),
                pltpu.VMEM(propagator.shape, bf16),
                pltpu.VMEM((n_wlk, occ + EXTRA, basis), bf16),
                pltpu.VMEM((basis, occ), bf16),
                pltpu.VMEM((n_vec, vecs * occ, basis), bf16),
                pltpu.VMEM((occ, basis), f32),
                dma((3,)),
                dma((others, pieces)), dma((others, chips, pieces)), dma((others,)), dma((others, chips)),
                dma((2 * chips + 1,)), dma, dma,
                regular((others,)), regular((chips,)), regular,
            ],
            compiler_params=pltpu.CompilerParams(
                collective_id=0, has_side_effects=True, vmem_limit_bytes=60000000),
        )(
            cholesky.reshape(vecs * occ, basis),
            orbitals.reshape(occ, basis),
            log_weights,
            parents,
            propagator,
        )

        def here(array):
            return pltpu.with_memory_space_constraint(array, pltpu.VMEM)

        out, log = pl.pallas_call(
            deliver,
            out_shape=(
                jax.ShapeDtypeStruct((occ, basis), f32),
                jax.ShapeDtypeStruct((1, 128), f32),
            ),
            in_specs=[vmem, vmem],
            out_specs=(hbm, hbm),
            scratch_shapes=[dma((2,))],
        )(here(x), here(logs))
        return out.reshape(orbitals.shape), log[0, :1]

    placed = (
        P(("grp", "vec"), None, None),
        P(("grp", "vec", "wlk"), None, None),
        P(("grp", "vec", "wlk")),
        P(("grp", "vec", "wlk")),
        P("grp", None),
    )
    return jax.shard_map(
        local,
        mesh=mesh,
        in_specs=placed,
        out_specs=(P(("grp", "vec", "wlk"), None, None), P(("grp", "vec", "wlk"))),
        check_vma=False,
    )
```

```python
import functools
import math

import jax
import jax.numpy as jnp
from jax import lax
from jax.experimental import pallas as pl
from jax.experimental.pallas import tpu as pltpu
from jax.sharding import PartitionSpec as P

NS_ITERS = 2

gradient_step = 0.25
energy_step = 0.002
epsilon = 1e-06

MESH = pl.DeviceIdType.MESH
UNROLL_LIMIT = 8
EXTRA = 16
ORDER = ((2, 3, 1), (0, 3, 2), (3, 0, 1), (2, 0, 1))


def dot(a, b):
    return lax.dot_general(a, b, (((1,), (0,)), ((), ())), preferred_element_type=jnp.float32)


def dot_t(a, b):
    return lax.dot_general(a, b, (((1,), (1,)), ((), ())), preferred_element_type=jnp.float32)


def each(count, body):
    if count <= UNROLL_LIMIT:
        for j in range(count):
            body(j)
    else:
        lax.fori_loop(0, count, lambda j, c: (body(j), c)[1], 0)


def kernel(
    n_vec, n_wlk, vecs, pieces, paired,
    chol_hbm, orb_hbm, logw, par, prop_hbm,
    out_ref, outlog_ref,
    orb, prop, propb, pop, turned, shared, acc, gsend, grecv,
    load_sem, z_recv, x_recv, near_recv, far_recv, p_recv, g_recv, v_send, p_send, g_send,
    z_ready, x_ready, sib_ready,
):
    me = lax.axis_index("vec")
    mw = lax.axis_index("wlk")
    occ, basis = orb.shape
    rows = vecs * occ
    share = rows // n_wlk
    step = share // pieces
    n_chip = n_wlk // 2
    chip, core = lax.div(mw, 2), lax.rem(mw, 2)
    sibling = mw + 1 - 2 * core
    others, chips = n_vec - 1, n_chip - 1
    scale = 1.0 / math.sqrt(vecs * n_vec)

    def remote(src_ref, dst_ref, send, recv, where):
        return pltpu.make_async_remote_copy(
            src_ref=src_ref, dst_ref=dst_ref, send_sem=send, recv_sem=recv,
            device_id=where, device_id_type=MESH)

    def at(w, k):
        return pl.ds(pl.multiple_of(w * share + k * step, step), step)

    def quarter(w):
        return pl.ds(pl.multiple_of(w * share, share), share)

    def slot(src, dst):
        return jnp.where(src > dst, src - 1, src)

    def peer(i):
        return lax.rem(chip + 1 + i, n_chip) * 2 + core

    def source(j):
        if n_vec == 4:
            first, *rest = (order[j] for order in ORDER)
            src = first
            for i, other in enumerate(rest):
                src = jnp.where(me == i + 1, other, src)
            return src
        lower = me - 1 - j
        return jnp.where(lower >= 0, lower, j + 1)

    def along(dst, k):
        return remote(chol_hbm.at[at(mw, k)], shared.at[me, at(mw, k)],
                      v_send, z_recv.at[slot(me, dst), k], {"vec": dst})

    def from_along(src, k):
        remote(shared.at[src, at(mw, k)], shared.at[src, at(mw, k)],
               v_send, z_recv.at[slot(src, me), k], {"wlk": sibling}).wait_recv()

    def across(src, i, k):
        return remote(shared.at[src, at(mw, k)], shared.at[src, at(mw, k)],
                      v_send, x_recv.at[slot(src, me), chips - 1 - i, k], {"wlk": peer(i)})

    def from_across(src, i, k):
        remote(shared.at[src, at(peer(i), k)], shared.at[src, at(peer(i), k)],
               v_send, x_recv.at[slot(src, me), i, k], {"wlk": sibling}).wait_recv()

    def beside(src, k):
        return remote(shared.at[src, at(mw, k)], shared.at[src, at(mw, k)],
                      v_send, near_recv.at[slot(src, me)], {"wlk": sibling})

    def from_beside(src):
        remote(shared.at[src, quarter(sibling)], shared.at[src, quarter(sibling)],
               v_send, near_recv.at[slot(src, me)], {"wlk": sibling}).wait_recv()

    def beyond(src, i, k):
        return remote(shared.at[src, at(peer(i), k)], shared.at[src, at(peer(i), k)],
                      v_send, far_recv.at[slot(src, me), i], {"wlk": sibling})

    def from_beyond(src, i):
        w = peer(i) + 1 - 2 * core
        remote(shared.at[src, quarter(w)], shared.at[src, quarter(w)],
               v_send, far_recv.at[slot(src, me), i], {"wlk": sibling}).wait_recv()

    def walker(w, index, where):
        return remote(pop.at[w], pop.at[w], p_send, p_recv.at[index], {"wlk": where})

    load_orb = pltpu.make_async_copy(orb_hbm, orb, load_sem.at[0])
    load_own = pltpu.make_async_copy(chol_hbm, shared.at[me], load_sem.at[1])
    load_prop = pltpu.make_async_copy(prop_hbm, prop, load_sem.at[2])

    barrier = pltpu.get_barrier_semaphore()

    def greet(semaphore, where):
        pl.semaphore_signal(semaphore, inc=1, device_id=where, device_id_type=MESH)

    each(others, lambda j: pl.when(j + 1 > me)(lambda: greet(barrier, {"vec": j + 1})))
    each(chips, lambda j: pl.when(j + 1 > chip)(
        lambda: greet(barrier, {"wlk": (j + 1) * 2 + core})))
    pl.when(core == 0)(lambda: greet(barrier, {"wlk": sibling}))

    load_orb.start()
    before = me + chip + core
    pl.when(before > 0)(lambda: pl.semaphore_wait(barrier, before))

    each(others, lambda j: pl.when(j < me)(lambda: greet(z_ready.at[me - 1], {"vec": j})))
    each(chips, lambda j: pl.when(j < chip)(
        lambda: greet(x_ready.at[chip - 1], {"wlk": j * 2 + core})))
    pl.when(core == 1)(lambda: greet(sib_ready, {"wlk": sibling}))

    def send_along(dst):
        for k in range(pieces):
            along(dst, k).start()

    if n_vec == 4:
        pl.when(me == 3)(lambda: send_along(2))
    each(others, lambda j: pl.when((j < me) & ((n_vec != 4) | (j != 2)))(lambda: send_along(j)))
    load_own.start()
    load_prop.start()

    def send_up(j):
        @pl.when(me + j + 1 < n_vec)
        def _():
            pl.semaphore_wait(z_ready.at[me + j], 1)
            send_along(me + j + 1)

    send_up(0)

    load_orb.wait()
    pop[mw, 0:occ] = orb[...].astype(jnp.bfloat16)
    whole = jnp.full((EXTRA, basis), logw[0], jnp.float32)
    high = whole.astype(jnp.bfloat16).astype(jnp.float32)
    middle = (whole - high).astype(jnp.bfloat16).astype(jnp.float32)
    low = whole - high - middle
    lane = lax.broadcasted_iota(jnp.int32, (EXTRA, basis), 1)
    parent = jnp.full((EXTRA, basis), par[0], jnp.int32).astype(jnp.float32)
    pop[mw, occ:occ + EXTRA] = jnp.where(
        lane == 0, high, jnp.where(lane == 1, middle, jnp.where(
            lane == 2, low, jnp.where(lane == 3, parent, 0.0)))).astype(jnp.bfloat16)

    pl.when(core == 0)(lambda: pl.semaphore_wait(sib_ready, 1))
    walker(mw, 2 * chips, sibling).start()
    each(chips, lambda j: pl.when(j + 1 > chip)(lambda: pl.semaphore_wait(x_ready.at[j], 1)))
    for i in range(chips):
        walker(mw, chips - 1 - i, peer(i)).start()

    def take(j, k):
        src = source(j)
        from_along(src, k)
        for i in range(chips):
            across(src, i, k).start()
        beside(src, k).start()

    def pass_on(j, k):
        src = source(j)
        for i in range(chips):
            from_across(src, i, k)
            beyond(src, i, k).start()

    def pass_walkers():
        for i in range(chips):
            walker(peer(i), i, sibling).wait_recv()
            walker(peer(i), chips + i, sibling).start()

    def all_walkers():
        for i in range(chips + 1):
            w = peer(i) + 1 - 2 * core
            walker(w, chips + i, sibling).wait_recv()

    row = lax.broadcasted_iota(jnp.int32, (occ, occ), 0)
    col = lax.broadcasted_iota(jnp.int32, (occ, occ), 1)
    diagonal = row == col

    def work(src, first, count):
        vectors = shared[src, pl.ds(pl.multiple_of(first * occ, occ), count * occ)]
        s = dot(vectors, turned[...])
        blocks = []
        for g in range(count):
            sg = s[g * occ:(g + 1) * occ, :]
            on_diagonal = jnp.where(diagonal, sg, 0.0)
            tg = jnp.sum(jnp.sum(on_diagonal, axis=0, keepdims=True), axis=1, keepdims=True)
            blocks.append((scale * (jnp.where(diagonal, tg, 0.0) - sg)).astype(jnp.bfloat16))
        adjoint = jnp.concatenate(blocks, axis=1) if count > 1 else blocks[0]
        acc[...] += dot(adjoint, vectors)

    def pick(w):
        parent = jnp.broadcast_to(pop[w, occ:occ + 1, 3:4].astype(jnp.float32), (occ + EXTRA, basis))
        picked = pop[0].astype(jnp.float32)
        for m in range(1, n_wlk):
            picked = jnp.where(parent == m, pop[m].astype(jnp.float32), picked)
        return picked

    def choose():
        picked = pick(mw)
        orb[...] = picked[0:occ]
        logs = picked[occ:occ + 8, 0:128]
        logs = jnp.where(lax.broadcasted_iota(jnp.int32, (8, 128), 1) < 3, logs, 0.0)
        outlog_ref[...] = jnp.broadcast_to(jnp.sum(logs, axis=1, keepdims=True), (8, 128))
        chosen = picked[0:occ]
        if paired:
            chosen = jnp.concatenate([chosen, pick(peer(0))[0:occ]], axis=0)
        turned[...] = chosen.T.astype(jnp.bfloat16)
        acc[...] = jnp.zeros_like(acc)

    def turn_propagator():
        load_prop.wait()
        propb[...] = prop[...].T.astype(jnp.bfloat16)

    half = vecs // 2
    where = lax.broadcasted_iota(jnp.int32, (occ, 2 * occ), 1)
    left = where < occ
    pair_diagonal = lax.broadcasted_iota(jnp.int32, (occ, 2 * occ), 0) == jnp.where(
        left, where, where - occ)

    def work_pair(src, last):
        vectors = shared[src, pl.ds(pl.multiple_of(chip * half * occ, occ), half * occ)]
        s = dot(vectors, turned[...])
        blocks = []
        for g in range(half):
            sg = s[g * occ:(g + 1) * occ, :]
            along_diagonal = jnp.sum(jnp.where(pair_diagonal, sg, 0.0), axis=0, keepdims=True)
            mine = jnp.sum(jnp.where(left[0:1], along_diagonal, 0.0), axis=1, keepdims=True)
            theirs = jnp.sum(jnp.where(left[0:1], 0.0, along_diagonal), axis=1, keepdims=True)
            trace = jnp.where(left, mine, theirs)
            blocks.append((scale * (jnp.where(pair_diagonal, trace, 0.0) - sg)).astype(jnp.bfloat16))
        mine = jnp.concatenate([b[:, 0:occ] for b in blocks], axis=1)
        theirs = jnp.concatenate([b[:, occ:] for b in blocks], axis=1)
        if last:
            gsend[...] = (acc[occ:] + dot(theirs, vectors)).astype(jnp.bfloat16)
            give().start()
            acc[0:occ] += dot(mine, vectors)
        else:
            acc[...] += dot(jnp.concatenate([mine, theirs], axis=0), vectors)

    def give():
        return remote(gsend, grecv, g_send, g_recv, {"wlk": peer(0)})

    if paired:
        for j in range(1, others):
            send_up(j)
        pass_walkers()
        turn_propagator()
        all_walkers()
        choose()
        load_own.wait()
        work_pair(me, False)
        for j in range(others):
            from_along(source(j), 0)
            beside(source(j), 0).start()
            if j > 0:
                from_beside(source(j - 1))
                work_pair(source(j - 1), False)
        from_beside(source(others - 1))
        work_pair(source(others - 1), True)
        give().wait_recv()
        acc[0:occ] += grecv[...].astype(jnp.float32)
    else:
        each(others - 1, lambda j: send_up(j + 1))
        pass_walkers()
        turn_propagator()
        all_walkers()
        choose()
        load_own.wait()
        work(me, 0, vecs)

        def one(j):
            for k in range(pieces):
                take(j, k)
            for k in range(pieces):
                pass_on(j, k)
            from_beside(source(j))
            for i in range(chips):
                from_beyond(source(j), i)
            work(source(j), 0, vecs)

        each(others, one)

    theta = orb[...]
    gradient = acc[0:occ]
    energy = 0.5 * jnp.sum(jnp.sum(theta * gradient, axis=0, keepdims=True), axis=1, keepdims=True)
    outlog_ref[...] -= energy_step * jnp.broadcast_to(energy, (8, 128))
    stepped = theta - gradient_step * gradient
    x = dot(stepped.astype(jnp.bfloat16), propb[...])
    mean_square = jnp.sum(jnp.sum(x * x, axis=0, keepdims=True), axis=1, keepdims=True)
    mean_square = mean_square / (occ * basis)
    norm = 1.0 / jnp.sqrt(mean_square + epsilon)
    for it in range(NS_ITERS):
        xb = x.astype(jnp.bfloat16)
        inter = dot_t(xb, xb) * (norm * norm / basis if it == 0 else 1.0 / basis)
        x = 0.5 * (3.0 * x - dot(inter.astype(jnp.bfloat16), xb))
        if it == 0:
            x = norm * x
    out_ref[...] = x

    def sent(view, semaphore):
        remote(view, view, semaphore, semaphore, {"wlk": sibling}).wait_send()

    if paired:
        sent(shared.at[pl.ds(0, others), pl.ds(0, 2 * share)], v_send)
        give().wait_send()
    else:
        sent(shared.at[pl.ds(0, others)], v_send)
    sent(pop.at[pl.ds(0, n_wlk - 1)], p_send)


def deliver(x_ref, log_ref, out_ref, outlog_ref, sem):
    copies = [
        pltpu.make_async_copy(log_ref.at[0:1], outlog_ref, sem.at[0]),
        pltpu.make_async_copy(x_ref, out_ref, sem.at[1]),
    ]
    for copy in copies:
        copy.start()
    for copy in copies:
        copy.wait()


def solution(mesh):
    n_vec, n_wlk = mesh.shape["vec"], mesh.shape["wlk"]

    def local(cholesky, orbitals, log_weights, parents, propagator):
        own, occ, basis = orbitals.shape
        assert own == 1 and n_wlk % 2 == 0
        vecs = cholesky.shape[0]
        share = vecs * occ // n_wlk
        assert share * n_wlk == vecs * occ
        paired = n_wlk == 4 and vecs % 2 == 0 and 2 <= n_vec <= UNROLL_LIMIT
        pieces, walkers = 1, 2 if paired else 1
        others, chips = n_vec - 1, n_wlk // 2 - 1
        crossing = (1, 1) if paired else (others, chips)
        f32, bf16 = jnp.float32, jnp.bfloat16
        dma = pltpu.SemaphoreType.DMA
        regular = pltpu.SemaphoreType.REGULAR
        hbm = pl.BlockSpec(memory_space=pltpu.HBM)
        smem = pl.BlockSpec(memory_space=pltpu.SMEM)
        vmem = pl.BlockSpec(memory_space=pltpu.VMEM)
        x, logs = pl.pallas_call(
            functools.partial(kernel, n_vec, n_wlk, vecs, pieces, paired),
            out_shape=(pltpu.VMEM((occ, basis), f32), pltpu.VMEM((8, 128), f32)),
            in_specs=[hbm, hbm, smem, smem, hbm],
            out_specs=(vmem, vmem),
            scratch_shapes=[
                pltpu.VMEM((occ, basis), f32),
                pltpu.VMEM(propagator.shape, f32),
                pltpu.VMEM(propagator.shape, bf16),
                pltpu.VMEM((n_wlk, occ + EXTRA, basis), bf16),
                pltpu.VMEM((basis, walkers * occ), bf16),
                pltpu.VMEM((n_vec, vecs * occ, basis), bf16),
                pltpu.VMEM((walkers * occ, basis), f32),
                pltpu.VMEM((occ, basis), bf16),
                pltpu.VMEM((occ, basis), bf16),
                dma((3,)),
                dma((others, pieces)), dma(crossing + (pieces,)), dma((others,)), dma(crossing),
                dma((2 * chips + 1,)), dma, dma, dma, dma,
                regular((others,)), regular((chips,)), regular,
            ],
            compiler_params=pltpu.CompilerParams(
                collective_id=0, has_side_effects=True, vmem_limit_bytes=60000000),
        )(
            cholesky.reshape(vecs * occ, basis),
            orbitals.reshape(occ, basis),
            log_weights,
            parents,
            propagator,
        )

        def here(array):
            return pltpu.with_memory_space_constraint(array, pltpu.VMEM)

        out, log = pl.pallas_call(
            deliver,
            out_shape=(
                jax.ShapeDtypeStruct((occ, basis), f32),
                jax.ShapeDtypeStruct((1, 128), f32),
            ),
            in_specs=[vmem, vmem],
            out_specs=(hbm, hbm),
            scratch_shapes=[dma((2,))],
        )(here(x), here(logs))
        return out.reshape(orbitals.shape), log[0, :1]

    placed = (
        P(("grp", "vec"), None, None),
        P(("grp", "vec", "wlk"), None, None),
        P(("grp", "vec", "wlk")),
        P(("grp", "vec", "wlk")),
        P("grp", None),
    )
    return jax.shard_map(
        local,
        mesh=mesh,
        in_specs=placed,
        out_specs=(P(("grp", "vec", "wlk"), None, None), P(("grp", "vec", "wlk"))),
        check_vma=False,
    )
```

```python
import functools
import math

import jax
import jax.numpy as jnp
from jax import lax
from jax.experimental import pallas as pl
from jax.experimental.pallas import tpu as pltpu
from jax.sharding import PartitionSpec as P

NS_ITERS = 2

gradient_step = 0.25
energy_step = 0.002
epsilon = 1e-06

MESH = pl.DeviceIdType.MESH
UNROLL_LIMIT = 8
EXTRA = 16
ORDER = ((3, 2, 1), (0, 3, 2), (0, 3, 1), (0, 1, 2))
WHOLE = tuple(order[-1] for order in ORDER)
BELOW = ((), (0,), (0, 1), (0, 2, 1))
ABOVE = ((2, 3, 1), (3, 2), (3,), ())
FULL_PIECES = 2


def dot(a, b):
    return lax.dot_general(a, b, (((1,), (0,)), ((), ())), preferred_element_type=jnp.float32)


def dot_t(a, b):
    return lax.dot_general(a, b, (((1,), (1,)), ((), ())), preferred_element_type=jnp.float32)


def each(count, body):
    if count <= UNROLL_LIMIT:
        for j in range(count):
            body(j)
    else:
        lax.fori_loop(0, count, lambda j, c: (body(j), c)[1], 0)


def kernel(
    n_vec, n_wlk, vecs, pieces, paired,
    chol_hbm, orb_hbm, logw, par, prop_hbm,
    out_ref, outlog_ref,
    orb, prop, propb, pop, turned, shared, acc, gsend, grecv,
    load_sem, z_recv, x_recv, near_recv, far_recv, p_recv, g_recv, v_send, p_send, g_send,
    z_ready, x_ready, sib_ready,
):
    me = lax.axis_index("vec")
    mw = lax.axis_index("wlk")
    occ, basis = orb.shape
    rows = vecs * occ
    share = rows // n_wlk
    step = share // pieces
    n_chip = n_wlk // 2
    chip, core = lax.div(mw, 2), lax.rem(mw, 2)
    sibling = mw + 1 - 2 * core
    others, chips = n_vec - 1, n_chip - 1
    scale = 1.0 / math.sqrt(vecs * n_vec)

    def remote(src_ref, dst_ref, send, recv, where):
        return pltpu.make_async_remote_copy(
            src_ref=src_ref, dst_ref=dst_ref, send_sem=send, recv_sem=recv,
            device_id=where, device_id_type=MESH)

    def at(w, k):
        return pl.ds(pl.multiple_of(w * share + k * step, step), step)

    def quarter(w):
        return pl.ds(pl.multiple_of(w * share, share), share)

    def slot(src, dst):
        return jnp.where(src > dst, src - 1, src)

    def peer(i):
        return lax.rem(chip + 1 + i, n_chip) * 2 + core

    def source(j):
        if paired:
            first, *rest = (order[j] for order in ORDER)
            src = first
            for i, other in enumerate(rest):
                src = jnp.where(me == i + 1, other, src)
            return src
        lower = me - 1 - j
        return jnp.where(lower >= 0, lower, j + 1)

    def along(dst, k):
        return remote(chol_hbm.at[at(mw, k)], shared.at[me, at(mw, k)],
                      v_send, z_recv.at[slot(me, dst), k], {"vec": dst})

    def from_along(src, k):
        remote(shared.at[src, at(mw, k)], shared.at[src, at(mw, k)],
               v_send, z_recv.at[slot(src, me), k], {"wlk": sibling}).wait_recv()

    def across(src, i, k):
        return remote(shared.at[src, at(mw, k)], shared.at[src, at(mw, k)],
                      v_send, x_recv.at[slot(src, me), chips - 1 - i, k], {"wlk": peer(i)})

    def from_across(src, i, k):
        remote(shared.at[src, at(peer(i), k)], shared.at[src, at(peer(i), k)],
               v_send, x_recv.at[slot(src, me), i, k], {"wlk": sibling}).wait_recv()

    def beside(src, k):
        return remote(shared.at[src, at(mw, k)], shared.at[src, at(mw, k)],
                      v_send, near_recv.at[slot(src, me)], {"wlk": sibling})

    def from_beside(src):
        remote(shared.at[src, quarter(sibling)], shared.at[src, quarter(sibling)],
               v_send, near_recv.at[slot(src, me)], {"wlk": sibling}).wait_recv()

    def beyond(src, i, k):
        return remote(shared.at[src, at(peer(i), k)], shared.at[src, at(peer(i), k)],
                      v_send, far_recv.at[slot(src, me), i], {"wlk": sibling})

    def from_beyond(src, i):
        w = peer(i) + 1 - 2 * core
        remote(shared.at[src, quarter(w)], shared.at[src, quarter(w)],
               v_send, far_recv.at[slot(src, me), i], {"wlk": sibling}).wait_recv()

    def walker(w, index, where):
        return remote(pop.at[w], pop.at[w], p_send, p_recv.at[index], {"wlk": where})

    load_orb = pltpu.make_async_copy(orb_hbm, orb, load_sem.at[0])
    load_own = pltpu.make_async_copy(chol_hbm, shared.at[me], load_sem.at[1])
    load_prop = pltpu.make_async_copy(prop_hbm, prop, load_sem.at[2])

    barrier = pltpu.get_barrier_semaphore()

    def greet(semaphore, where):
        pl.semaphore_signal(semaphore, inc=1, device_id=where, device_id_type=MESH)

    each(others, lambda j: pl.when(j + 1 > me)(lambda: greet(barrier, {"vec": j + 1})))
    each(chips, lambda j: pl.when(j + 1 > chip)(
        lambda: greet(barrier, {"wlk": (j + 1) * 2 + core})))
    pl.when(core == 0)(lambda: greet(barrier, {"wlk": sibling}))

    load_orb.start()
    before = me + chip + core
    pl.when(before > 0)(lambda: pl.semaphore_wait(barrier, before))

    each(others, lambda j: pl.when(j < me)(lambda: greet(z_ready.at[me - 1], {"vec": j})))
    each(chips, lambda j: pl.when(j < chip)(
        lambda: greet(x_ready.at[chip - 1], {"wlk": j * 2 + core})))
    pl.when(core == 1)(lambda: greet(sib_ready, {"wlk": sibling}))

    def send_along(dst):
        for k in range(pieces):
            along(dst, k).start()

    def send_up(j):
        @pl.when(me + j + 1 < n_vec)
        def _():
            pl.semaphore_wait(z_ready.at[me + j], 1)
            send_along(me + j + 1)

    def core_rows(c, k):
        part = rows // (2 * FULL_PIECES)
        return pl.ds(pl.multiple_of((c * FULL_PIECES + k) * part, part), part)

    def along_whole(src, dst, k):
        return remote(chol_hbm.at[core_rows(core, k)], shared.at[src, core_rows(core, k)],
                      v_send, z_recv.at[src - (src > dst), k], {"vec": dst})

    def send(src, dst):
        if dst > src:
            pl.semaphore_wait(z_ready.at[dst - 1], 1)
        if WHOLE[dst] == src:
            for k in range(FULL_PIECES):
                along_whole(src, dst, k).start()
        else:
            remote(chol_hbm.at[quarter(mw)], shared.at[src, quarter(mw)],
                   v_send, z_recv.at[src - (src > dst), 0], {"vec": dst}).start()

    def send_all(plan):
        for v in range(n_vec):
            @pl.when(me == v)
            def _():
                for d in plan[v]:
                    send(v, d)

    if paired:
        send_all(BELOW)
    else:
        each(others, lambda j: pl.when(j < me)(lambda: send_along(j)))
    load_own.start()
    load_prop.start()

    load_orb.wait()
    pop[mw, 0:occ] = orb[...].astype(jnp.bfloat16)
    whole = jnp.full((EXTRA, basis), logw[0], jnp.float32)
    high = whole.astype(jnp.bfloat16).astype(jnp.float32)
    middle = (whole - high).astype(jnp.bfloat16).astype(jnp.float32)
    low = whole - high - middle
    lane = lax.broadcasted_iota(jnp.int32, (EXTRA, basis), 1)
    parent = jnp.full((EXTRA, basis), par[0], jnp.int32).astype(jnp.float32)
    pop[mw, occ:occ + EXTRA] = jnp.where(
        lane == 0, high, jnp.where(lane == 1, middle, jnp.where(
            lane == 2, low, jnp.where(lane == 3, parent, 0.0)))).astype(jnp.bfloat16)

    pl.when(core == 0)(lambda: pl.semaphore_wait(sib_ready, 1))
    walker(mw, 2 * chips, sibling).start()
    if paired:
        pl.when(chip == 1)(lambda: walker(mw, 0, peer(0)).start())
        send_all([d[:1] for d in ABOVE])

        @pl.when(chip == 0)
        def _():
            pl.semaphore_wait(x_ready.at[0], 1)
            walker(mw, 0, peer(0)).start()

        send_all([d[1:] for d in ABOVE])
    else:
        each(chips, lambda j: pl.when(j + 1 > chip)(lambda: pl.semaphore_wait(x_ready.at[j], 1)))
        for i in range(chips):
            walker(mw, chips - 1 - i, peer(i)).start()
        each(others, send_up)

    def take(j, k):
        src = source(j)
        from_along(src, k)
        for i in range(chips):
            across(src, i, k).start()
        beside(src, k).start()

    def pass_on(j, k):
        src = source(j)
        for i in range(chips):
            from_across(src, i, k)
            beyond(src, i, k).start()

    def pass_walkers():
        for i in range(chips):
            walker(peer(i), i, sibling).wait_recv()
            walker(peer(i), chips + i, sibling).start()

    def all_walkers():
        for i in range(chips + 1):
            w = peer(i) + 1 - 2 * core
            walker(w, chips + i, sibling).wait_recv()

    row = lax.broadcasted_iota(jnp.int32, (occ, occ), 0)
    col = lax.broadcasted_iota(jnp.int32, (occ, occ), 1)
    diagonal = row == col

    def work(src, first, count):
        vectors = shared[src, pl.ds(pl.multiple_of(first * occ, occ), count * occ)]
        s = dot(vectors, turned[:, 0:occ])
        blocks = []
        for g in range(count):
            sg = s[g * occ:(g + 1) * occ, :]
            on_diagonal = jnp.where(diagonal, sg, 0.0)
            tg = jnp.sum(jnp.sum(on_diagonal, axis=0, keepdims=True), axis=1, keepdims=True)
            blocks.append((scale * (jnp.where(diagonal, tg, 0.0) - sg)).astype(jnp.bfloat16))
        adjoint = jnp.concatenate(blocks, axis=1) if count > 1 else blocks[0]
        acc[0:occ] += dot(adjoint, vectors)

    def pick(w):
        parent = jnp.broadcast_to(pop[w, occ:occ + 1, 3:4].astype(jnp.float32), (occ + EXTRA, basis))
        picked = pop[0].astype(jnp.float32)
        for m in range(1, n_wlk):
            picked = jnp.where(parent == m, pop[m].astype(jnp.float32), picked)
        return picked

    def choose():
        picked = pick(mw)
        orb[...] = picked[0:occ]
        logs = picked[occ:occ + 8, 0:128]
        logs = jnp.where(lax.broadcasted_iota(jnp.int32, (8, 128), 1) < 3, logs, 0.0)
        outlog_ref[...] = jnp.broadcast_to(jnp.sum(logs, axis=1, keepdims=True), (8, 128))
        chosen = picked[0:occ]
        if paired:
            chosen = jnp.concatenate([chosen, pick(peer(0))[0:occ]], axis=0)
        turned[...] = chosen.T.astype(jnp.bfloat16)
        acc[...] = jnp.zeros_like(acc)

    def turn_propagator():
        load_prop.wait()
        propb[...] = prop[...].T.astype(jnp.bfloat16)

    half = vecs // 2
    where = lax.broadcasted_iota(jnp.int32, (occ, 2 * occ), 1)
    left = where < occ
    pair_diagonal = lax.broadcasted_iota(jnp.int32, (occ, 2 * occ), 0) == jnp.where(
        left, where, where - occ)

    def work_pair(src, last):
        vectors = shared[src, pl.ds(pl.multiple_of(chip * half * occ, occ), half * occ)]
        s = dot(vectors, turned[...])
        blocks = []
        for g in range(half):
            sg = s[g * occ:(g + 1) * occ, :]
            along_diagonal = jnp.sum(jnp.where(pair_diagonal, sg, 0.0), axis=0, keepdims=True)
            mine = jnp.sum(jnp.where(left[0:1], along_diagonal, 0.0), axis=1, keepdims=True)
            theirs = jnp.sum(jnp.where(left[0:1], 0.0, along_diagonal), axis=1, keepdims=True)
            trace = jnp.where(left, mine, theirs)
            blocks.append((scale * (jnp.where(pair_diagonal, trace, 0.0) - sg)).astype(jnp.bfloat16))
        mine = jnp.concatenate([b[:, 0:occ] for b in blocks], axis=1)
        theirs = jnp.concatenate([b[:, occ:] for b in blocks], axis=1)
        if last:
            gsend[...] = (acc[occ:] + dot(theirs, vectors)).astype(jnp.bfloat16)
            give().start()
            acc[0:occ] += dot(mine, vectors)
        else:
            acc[...] += dot(jnp.concatenate([mine, theirs], axis=0), vectors)

    def give():
        return remote(gsend, grecv, g_send, g_recv, {"wlk": peer(0)})

    if paired:
        pass_walkers()
        turn_propagator()
        all_walkers()
        choose()
        load_own.wait()
        work_pair(me, False)
        for j in range(others - 1):
            from_along(source(j), 0)
            beside(source(j), 0).start()
            if j > 0:
                from_beside(source(j - 1))
                work_pair(source(j - 1), False)
        from_beside(source(others - 2))
        work_pair(source(others - 2), True)
        final = source(others - 1)
        for k in range(FULL_PIECES):
            view = shared.at[final, core_rows(core, k)]
            remote(view, view, v_send, z_recv.at[slot(final, me), k], {"wlk": sibling}).wait_recv()
            remote(view, view, v_send, near_recv.at[slot(final, me)], {"wlk": sibling}).start()
        work(final, core * half, half)
        view = shared.at[final, pl.ds(pl.multiple_of((1 - core) * (rows // 2), rows // 2), rows // 2)]
        remote(view, view, v_send, near_recv.at[slot(final, me)], {"wlk": sibling}).wait_recv()
        work(final, (1 - core) * half, half)
        give().wait_recv()
        acc[0:occ] += grecv[...].astype(jnp.float32)
    else:
        pass_walkers()
        turn_propagator()
        all_walkers()
        choose()
        load_own.wait()
        work(me, 0, vecs)

        def one(j):
            for k in range(pieces):
                take(j, k)
            for k in range(pieces):
                pass_on(j, k)
            from_beside(source(j))
            for i in range(chips):
                from_beyond(source(j), i)
            work(source(j), 0, vecs)

        each(others, one)

    theta = orb[...]
    gradient = acc[0:occ]
    energy = 0.5 * jnp.sum(jnp.sum(theta * gradient, axis=0, keepdims=True), axis=1, keepdims=True)
    outlog_ref[...] -= energy_step * jnp.broadcast_to(energy, (8, 128))
    stepped = theta - gradient_step * gradient
    x = dot(stepped.astype(jnp.bfloat16), propb[...])
    mean_square = jnp.sum(jnp.sum(x * x, axis=0, keepdims=True), axis=1, keepdims=True)
    mean_square = mean_square / (occ * basis)
    norm = 1.0 / jnp.sqrt(mean_square + epsilon)
    for it in range(NS_ITERS):
        xb = x.astype(jnp.bfloat16)
        inter = dot_t(xb, xb) * (norm * norm / basis if it == 0 else 1.0 / basis)
        x = 0.5 * (3.0 * x - dot(inter.astype(jnp.bfloat16), xb))
        if it == 0:
            x = norm * x
    out_ref[...] = x

    def sent(view, semaphore):
        remote(view, view, semaphore, semaphore, {"wlk": sibling}).wait_send()

    def moved(v):
        total = sum(rows // 2 if WHOLE[d] == v else share for d in range(n_vec) if d != v)
        return (total + (others - 1) * share + rows // 2) // others

    if paired:
        for v in range(n_vec):
            view = shared.at[pl.ds(0, others), pl.ds(0, moved(v))]
            pl.when(me == v)(functools.partial(sent, view, v_send))
        give().wait_send()
    else:
        sent(shared.at[pl.ds(0, others)], v_send)
    sent(pop.at[pl.ds(0, n_wlk - 1)], p_send)


def deliver(x_ref, log_ref, out_ref, outlog_ref, sem):
    copies = [
        pltpu.make_async_copy(log_ref.at[0:1], outlog_ref, sem.at[0]),
        pltpu.make_async_copy(x_ref, out_ref, sem.at[1]),
    ]
    for copy in copies:
        copy.start()
    for copy in copies:
        copy.wait()


def solution(mesh):
    n_vec, n_wlk = mesh.shape["vec"], mesh.shape["wlk"]

    def local(cholesky, orbitals, log_weights, parents, propagator):
        own, occ, basis = orbitals.shape
        assert own == 1 and n_wlk % 2 == 0
        vecs = cholesky.shape[0]
        share = vecs * occ // n_wlk
        assert share * n_wlk == vecs * occ
        paired = n_wlk == 4 and n_vec == 4 and vecs % 2 == 0
        pieces, walkers = 1, 2 if paired else 1
        others, chips = n_vec - 1, n_wlk // 2 - 1
        crossing = (1, 1) if paired else (others, chips)
        f32, bf16 = jnp.float32, jnp.bfloat16
        dma = pltpu.SemaphoreType.DMA
        regular = pltpu.SemaphoreType.REGULAR
        hbm = pl.BlockSpec(memory_space=pltpu.HBM)
        smem = pl.BlockSpec(memory_space=pltpu.SMEM)
        vmem = pl.BlockSpec(memory_space=pltpu.VMEM)
        x, logs = pl.pallas_call(
            functools.partial(kernel, n_vec, n_wlk, vecs, pieces, paired),
            out_shape=(pltpu.VMEM((occ, basis), f32), pltpu.VMEM((8, 128), f32)),
            in_specs=[hbm, hbm, smem, smem, hbm],
            out_specs=(vmem, vmem),
            scratch_shapes=[
                pltpu.VMEM((occ, basis), f32),
                pltpu.VMEM(propagator.shape, f32),
                pltpu.VMEM(propagator.shape, bf16),
                pltpu.VMEM((n_wlk, occ + EXTRA, basis), bf16),
                pltpu.VMEM((basis, walkers * occ), bf16),
                pltpu.VMEM((n_vec, vecs * occ, basis), bf16),
                pltpu.VMEM((walkers * occ, basis), f32),
                pltpu.VMEM((occ, basis), bf16),
                pltpu.VMEM((occ, basis), bf16),
                dma((3,)),
                dma((others, FULL_PIECES)), dma(crossing + (pieces,)), dma((others,)), dma(crossing),
                dma((2 * chips + 1,)), dma, dma, dma, dma,
                regular((others,)), regular((chips,)), regular,
            ],
            compiler_params=pltpu.CompilerParams(
                collective_id=0, has_side_effects=True, vmem_limit_bytes=60000000),
        )(
            cholesky.reshape(vecs * occ, basis),
            orbitals.reshape(occ, basis),
            log_weights,
            parents,
            propagator,
        )

        def here(array):
            return pltpu.with_memory_space_constraint(array, pltpu.VMEM)

        out, log = pl.pallas_call(
            deliver,
            out_shape=(
                jax.ShapeDtypeStruct((occ, basis), f32),
                jax.ShapeDtypeStruct((1, 128), f32),
            ),
            in_specs=[vmem, vmem],
            out_specs=(hbm, hbm),
            scratch_shapes=[dma((2,))],
        )(here(x), here(logs))
        return out.reshape(orbitals.shape), log[0, :1]

    placed = (
        P(("grp", "vec"), None, None),
        P(("grp", "vec", "wlk"), None, None),
        P(("grp", "vec", "wlk")),
        P(("grp", "vec", "wlk")),
        P("grp", None),
    )
    return jax.shard_map(
        local,
        mesh=mesh,
        in_specs=placed,
        out_specs=(P(("grp", "vec", "wlk"), None, None), P(("grp", "vec", "wlk"))),
        check_vma=False,
    )
```

```python
import functools
import math

import jax
import jax.numpy as jnp
from jax import lax
from jax.experimental import pallas as pl
from jax.experimental.pallas import tpu as pltpu
from jax.sharding import PartitionSpec as P

NS_ITERS = 2

gradient_step = 0.25
energy_step = 0.002
epsilon = 1e-06

MESH = pl.DeviceIdType.MESH
UNROLL_LIMIT = 8
EXTRA = 16
ORDER = ((3, 2, 1), (0, 3, 2), (0, 3, 1), (0, 1, 2))
WHOLE = tuple(order[-1] for order in ORDER)
BELOW = ((), ((0,),), ((0,),), ((0,), (2,), (1,)))
ABOVE = (((2,), (3,), (1,)), ((2, True, False), (3,)), ((3,),), ())
LATE = ((), ((2, False, True),), ((1,),), ())
FULL_PIECES = 3
MIXED = (False, False, True, False)
LEAN = 0


def dot(a, b):
    return lax.dot_general(a, b, (((1,), (0,)), ((), ())), preferred_element_type=jnp.float32)


def dot_t(a, b):
    return lax.dot_general(a, b, (((1,), (1,)), ((), ())), preferred_element_type=jnp.float32)


def each(count, body):
    if count <= UNROLL_LIMIT:
        for j in range(count):
            body(j)
    else:
        lax.fori_loop(0, count, lambda j, c: (body(j), c)[1], 0)


def kernel(
    n_vec, n_wlk, vecs, pieces, paired,
    chol_hbm, orb_hbm, logw, par, prop_hbm,
    out_ref, outlog_ref,
    orb, prop, propb, pop, turned, shared, acc, gsend, grecv,
    load_sem, z_recv, x_recv, near_recv, far_recv, p_recv, g_recv, v_send, p_send, g_send, odd_send, last_recv,
    z_ready, x_ready, sib_ready,
):
    me = lax.axis_index("vec")
    mw = lax.axis_index("wlk")
    occ, basis = orb.shape
    rows = vecs * occ
    share = rows // n_wlk
    step = share // pieces
    n_chip = n_wlk // 2
    chip, core = lax.div(mw, 2), lax.rem(mw, 2)
    sibling = mw + 1 - 2 * core
    others, chips = n_vec - 1, n_chip - 1
    half = vecs // 2
    scale = 1.0 / math.sqrt(vecs * n_vec)

    def remote(src_ref, dst_ref, send, recv, where):
        return pltpu.make_async_remote_copy(
            src_ref=src_ref, dst_ref=dst_ref, send_sem=send, recv_sem=recv,
            device_id=where, device_id_type=MESH)

    def at(w, k):
        return pl.ds(pl.multiple_of(w * share + k * step, step), step)

    def quarter(w):
        return pl.ds(pl.multiple_of(w * share, share), share)

    def slot(src, dst):
        return jnp.where(src > dst, src - 1, src)

    def peer(i):
        return lax.rem(chip + 1 + i, n_chip) * 2 + core

    def source(j):
        if paired:
            first, *rest = (order[j] for order in ORDER)
            src = first
            for i, other in enumerate(rest):
                src = jnp.where(me == i + 1, other, src)
            return src
        lower = me - 1 - j
        return jnp.where(lower >= 0, lower, j + 1)

    def along(dst, k):
        return remote(chol_hbm.at[at(mw, k)], shared.at[me, at(mw, k)],
                      v_send, z_recv.at[slot(me, dst), k], {"vec": dst})

    def from_along(src, k):
        remote(shared.at[src, at(mw, k)], shared.at[src, at(mw, k)],
               v_send, z_recv.at[slot(src, me), k], {"wlk": sibling}).wait_recv()

    def across(src, i, k):
        return remote(shared.at[src, at(mw, k)], shared.at[src, at(mw, k)],
                      v_send, x_recv.at[slot(src, me), chips - 1 - i, k], {"wlk": peer(i)})

    def from_across(src, i, k):
        remote(shared.at[src, at(peer(i), k)], shared.at[src, at(peer(i), k)],
               v_send, x_recv.at[slot(src, me), i, k], {"wlk": sibling}).wait_recv()

    def beside(src, k):
        return remote(shared.at[src, at(mw, k)], shared.at[src, at(mw, k)],
                      v_send, near_recv.at[slot(src, me)], {"wlk": sibling})

    def from_beside(src):
        remote(shared.at[src, quarter(sibling)], shared.at[src, quarter(sibling)],
               v_send, near_recv.at[slot(src, me)], {"wlk": sibling}).wait_recv()

    def beyond(src, i, k):
        return remote(shared.at[src, at(peer(i), k)], shared.at[src, at(peer(i), k)],
                      v_send, far_recv.at[slot(src, me), i], {"wlk": sibling})

    def from_beyond(src, i):
        w = peer(i) + 1 - 2 * core
        remote(shared.at[src, quarter(w)], shared.at[src, quarter(w)],
               v_send, far_recv.at[slot(src, me), i], {"wlk": sibling}).wait_recv()

    def walker(w, index, where):
        return remote(pop.at[w], pop.at[w], p_send, p_recv.at[index], {"wlk": where})

    load_orb = pltpu.make_async_copy(orb_hbm, orb, load_sem.at[0])
    load_own = pltpu.make_async_copy(chol_hbm, shared.at[me], load_sem.at[1])
    load_prop = pltpu.make_async_copy(prop_hbm, prop, load_sem.at[2])

    barrier = pltpu.get_barrier_semaphore()

    def greet(semaphore, where):
        pl.semaphore_signal(semaphore, inc=1, device_id=where, device_id_type=MESH)

    each(others, lambda j: pl.when(j + 1 > me)(lambda: greet(barrier, {"vec": j + 1})))
    each(chips, lambda j: pl.when(j + 1 > chip)(
        lambda: greet(barrier, {"wlk": (j + 1) * 2 + core})))
    pl.when(core == 0)(lambda: greet(barrier, {"wlk": sibling}))

    load_orb.start()
    before = me + chip + core
    pl.when(before > 0)(lambda: pl.semaphore_wait(barrier, before))

    each(others, lambda j: pl.when(j < me)(lambda: greet(z_ready.at[me - 1], {"vec": j})))
    each(chips, lambda j: pl.when(j < chip)(
        lambda: greet(x_ready.at[chip - 1], {"wlk": j * 2 + core})))
    pl.when(core == 1)(lambda: greet(sib_ready, {"wlk": sibling}))

    def send_along(dst):
        for k in range(pieces):
            along(dst, k).start()

    def send_up(j):
        @pl.when(me + j + 1 < n_vec)
        def _():
            pl.semaphore_wait(z_ready.at[me + j], 1)
            send_along(me + j + 1)

    batch = vecs // FULL_PIECES
    alone = (FULL_PIECES - 1) * batch

    def whole_parts(v):
        parts = [(k * batch, batch) for k in range(FULL_PIECES)]
        return parts[:-1] + [(alone + 1, batch - 1)] if MIXED[v] else parts

    def core_rows(c, begin, count):
        part = count * occ // 2
        return pl.ds(pl.multiple_of(begin * occ + c * part, part), part)

    def to_core(src, dst, begin, count, k):
        remote(chol_hbm.at[core_rows(core, begin, count)], shared.at[src, core_rows(core, begin, count)],
               v_send, z_recv.at[2 + k, 0], {"vec": dst}).start()

    def halves(v, c):
        if v == 0:
            cut = min(half + LEAN, vecs - 1)
            return (cut, vecs - cut) if c else (0, cut)
        return c * half, half

    def core_part(v, c, k):
        begin, count = halves(v, c)
        part = count * occ // 2
        return pl.ds(pl.multiple_of(begin * occ + k * part, part), part)

    def send_part(src, dst, c):
        remote(chol_hbm.at[core_part(dst, c, core)], shared.at[src, core_part(dst, c, core)],
               v_send if dst else odd_send, z_recv.at[ORDER[dst].index(src), 0], {"vec": dst}).start()

    def send(src, dst, some=True, rest=True):
        if dst > src and some:
            pl.semaphore_wait(z_ready.at[dst - 1], 1)
        if WHOLE[dst] == src:
            if some and MIXED[dst]:
                pl.when(chip == 0)(lambda: to_core(src, dst, alone, 1, FULL_PIECES))
            for k, part in enumerate(whole_parts(dst) if rest else ()):
                to_core(src, dst, *part, k)
        else:
            for c in range(2):
                pl.when(chip == c)(functools.partial(send_part, src, dst, c))

    def send_all(plan):
        for v in range(n_vec):
            @pl.when(me == v)
            def _():
                for d in plan[v]:
                    send(v, *d)

    if paired:
        send_all(BELOW)
    else:
        each(others, lambda j: pl.when(j < me)(lambda: send_along(j)))
    load_own.start()
    load_prop.start()

    load_orb.wait()
    pop[mw, 0:occ] = orb[...].astype(jnp.bfloat16)
    whole = jnp.full((EXTRA, basis), logw[0], jnp.float32)
    high = whole.astype(jnp.bfloat16).astype(jnp.float32)
    middle = (whole - high).astype(jnp.bfloat16).astype(jnp.float32)
    low = whole - high - middle
    lane = lax.broadcasted_iota(jnp.int32, (EXTRA, basis), 1)
    parent = jnp.full((EXTRA, basis), par[0], jnp.int32).astype(jnp.float32)
    pop[mw, occ:occ + EXTRA] = jnp.where(
        lane == 0, high, jnp.where(lane == 1, middle, jnp.where(
            lane == 2, low, jnp.where(lane == 3, parent, 0.0)))).astype(jnp.bfloat16)

    pl.when(core == 0)(lambda: pl.semaphore_wait(sib_ready, 1))
    walker(mw, 2 * chips, sibling).start()
    if paired:
        pl.when(chip == 1)(lambda: walker(mw, 0, peer(0)).start())
        send_all([d[:1] for d in ABOVE])

        @pl.when(chip == 0)
        def _():
            pl.semaphore_wait(x_ready.at[0], 1)
            walker(mw, 0, peer(0)).start()

        send_all([d[1:] for d in ABOVE])
    else:
        each(chips, lambda j: pl.when(j + 1 > chip)(lambda: pl.semaphore_wait(x_ready.at[j], 1)))
        for i in range(chips):
            walker(mw, chips - 1 - i, peer(i)).start()
        each(others, send_up)

    def take(j, k):
        src = source(j)
        from_along(src, k)
        for i in range(chips):
            across(src, i, k).start()
        beside(src, k).start()

    def pass_on(j, k):
        src = source(j)
        for i in range(chips):
            from_across(src, i, k)
            beyond(src, i, k).start()

    def pass_walkers():
        for i in range(chips):
            walker(peer(i), i, sibling).wait_recv()
            walker(peer(i), chips + i, sibling).start()

    def all_walkers():
        for i in range(chips + 1):
            w = peer(i) + 1 - 2 * core
            walker(w, chips + i, sibling).wait_recv()

    row = lax.broadcasted_iota(jnp.int32, (occ, occ), 0)
    col = lax.broadcasted_iota(jnp.int32, (occ, occ), 1)
    diagonal = row == col

    def work(src, first, count):
        vectors = shared[src, pl.ds(pl.multiple_of(first * occ, occ), count * occ)]
        s = dot(vectors, turned[:, 0:occ])
        swapped = (-scale * s).astype(jnp.bfloat16)
        blocks = [swapped[g * occ:(g + 1) * occ, :] for g in range(count)]
        direct = jnp.zeros((occ, basis), jnp.float32)
        for g in range(count):
            on_diagonal = jnp.where(diagonal, s[g * occ:(g + 1) * occ, :], 0.0)
            tg = jnp.sum(jnp.sum(on_diagonal, axis=0, keepdims=True), axis=1, keepdims=True)
            direct += (scale * tg) * vectors[g * occ:(g + 1) * occ].astype(jnp.float32)
        adjoint = jnp.concatenate(blocks, axis=1) if count > 1 else blocks[0]
        acc[0:occ] += dot(adjoint, vectors) + direct

    def pick(w):
        parent = jnp.broadcast_to(pop[w, occ:occ + 1, 3:4].astype(jnp.float32), (occ + EXTRA, basis))
        picked = pop[0].astype(jnp.float32)
        for m in range(1, n_wlk):
            picked = jnp.where(parent == m, pop[m].astype(jnp.float32), picked)
        return picked

    def choose():
        picked = pick(mw)
        orb[...] = picked[0:occ]
        logs = picked[occ:occ + 8, 0:128]
        logs = jnp.where(lax.broadcasted_iota(jnp.int32, (8, 128), 1) < 3, logs, 0.0)
        outlog_ref[...] = jnp.broadcast_to(jnp.sum(logs, axis=1, keepdims=True), (8, 128))
        chosen = picked[0:occ]
        if paired:
            chosen = jnp.concatenate([chosen, pick(peer(0))[0:occ]], axis=0)
        turned[...] = chosen.T.astype(jnp.bfloat16)
        acc[...] = jnp.zeros_like(acc)

    def turn_propagator():
        load_prop.wait()
        propb[...] = prop[...].T.astype(jnp.bfloat16)

    where = lax.broadcasted_iota(jnp.int32, (occ, 2 * occ), 1)
    left = where < occ
    pair_diagonal = lax.broadcasted_iota(jnp.int32, (occ, 2 * occ), 0) == jnp.where(
        left, where, where - occ)

    def work_pair(src, begin, count, last):
        vectors = shared[src, pl.ds(pl.multiple_of(begin * occ, occ), count * occ)]
        s = dot(vectors, turned[...])
        swapped = (-scale * s).astype(jnp.bfloat16)
        blocks = [swapped[g * occ:(g + 1) * occ, :] for g in range(count)]
        direct = [jnp.zeros((occ, basis), jnp.float32)] * 2
        for g in range(count):
            sg = s[g * occ:(g + 1) * occ, :]
            along_diagonal = jnp.sum(jnp.where(pair_diagonal, sg, 0.0), axis=0, keepdims=True)
            block = vectors[g * occ:(g + 1) * occ].astype(jnp.float32)
            for i in range(2):
                side = jnp.where(left[0:1] if i == 0 else jnp.logical_not(left[0:1]), along_diagonal, 0.0)
                direct[i] = direct[i] + scale * jnp.sum(side, axis=1, keepdims=True) * block
        mine = jnp.concatenate([b[:, 0:occ] for b in blocks], axis=1)
        theirs = jnp.concatenate([b[:, occ:] for b in blocks], axis=1)
        if last:
            gsend[...] = (acc[occ:] + dot(theirs, vectors) + direct[1]).astype(jnp.bfloat16)
            give().start()
            acc[0:occ] += dot(mine, vectors) + direct[0]
        else:
            acc[...] += dot(jnp.concatenate([mine, theirs], axis=0), vectors) + jnp.concatenate(
                direct, axis=0)

    def gather(v, c):
        semaphore = v_send if v else odd_send
        first, second, final = ORDER[v]

        def landed(view, signal):
            remote(view, view, v_send, signal, {"wlk": sibling}).wait_recv()

        def pass_beside(view, send, signal):
            remote(view, view, send, signal, {"wlk": sibling}).start()

        def take(src):
            view = shared.at[src, core_part(v, c, core)]
            landed(view, z_recv.at[ORDER[v].index(src), 0])
            pass_beside(view, semaphore, near_recv.at[src - (src > v)])

        def finish(src, last):
            landed(shared.at[src, core_part(v, c, 1 - core)], near_recv.at[src - (src > v)])
            work_pair(src, *halves(v, c), last)

        at_final = final - (final > v)
        mixed = MIXED[v] and c == 0
        take(first)
        take(second)
        finish(first, False)
        finish(second, not mixed)
        if mixed:
            view = shared.at[final, core_rows(core, alone, 1)]
            landed(view, z_recv.at[2 + FULL_PIECES, 0])
            pass_beside(view, v_send, near_recv.at[at_final])
            landed(shared.at[final, core_rows(1 - core, alone, 1)], near_recv.at[at_final])
            work_pair(final, alone, 1, True)
        parts = whole_parts(v)
        for k in range(FULL_PIECES + 1):
            if k < FULL_PIECES:
                view = shared.at[final, core_rows(core, *parts[k])]
                landed(view, z_recv.at[2 + k, 0])
                pass_beside(view, v_send, last_recv.at[k])
            if k > 0:
                landed(shared.at[final, core_rows(1 - core, *parts[k - 1])], last_recv.at[k - 1])
                work(final, *parts[k - 1])

    def give():
        return remote(gsend, grecv, g_send, g_recv, {"wlk": peer(0)})

    if paired:
        pass_walkers()
        send_all(LATE)
        turn_propagator()
        all_walkers()
        choose()
        load_own.wait()
        work_pair(me, chip * half, half, False)
        for v in range(n_vec):
            for c in range(2):
                pl.when((me == v) & (chip == c))(functools.partial(gather, v, c))
        give().wait_recv()
        acc[0:occ] += grecv[...].astype(jnp.float32)
    else:
        pass_walkers()
        turn_propagator()
        all_walkers()
        choose()
        load_own.wait()
        work(me, 0, vecs)

        def one(j):
            for k in range(pieces):
                take(j, k)
            for k in range(pieces):
                pass_on(j, k)
            from_beside(source(j))
            for i in range(chips):
                from_beyond(source(j), i)
            work(source(j), 0, vecs)

        each(others, one)

    theta = orb[...]
    gradient = acc[0:occ]
    energy = 0.5 * jnp.sum(jnp.sum(theta * gradient, axis=0, keepdims=True), axis=1, keepdims=True)
    outlog_ref[...] -= energy_step * jnp.broadcast_to(energy, (8, 128))
    stepped = theta - gradient_step * gradient
    x = dot(stepped.astype(jnp.bfloat16), propb[...])
    mean_square = jnp.sum(jnp.sum(x * x, axis=0, keepdims=True), axis=1, keepdims=True)
    mean_square = mean_square / (occ * basis)
    norm = 1.0 / jnp.sqrt(mean_square + epsilon)
    for it in range(NS_ITERS):
        xb = x.astype(jnp.bfloat16)
        inter = dot_t(xb, xb) * (norm * norm / basis if it == 0 else 1.0 / basis)
        x = 0.5 * (3.0 * x - dot(inter.astype(jnp.bfloat16), xb))
        if it == 0:
            x = norm * x
    out_ref[...] = x

    def sent(view, semaphore):
        remote(view, view, semaphore, semaphore, {"wlk": sibling}).wait_send()

    def whole_rows(v, c):
        return (rows - (occ if MIXED[v] and c else 0)) // 2

    def moved(v, c):
        total = sum(whole_rows(d, c) if WHOLE[d] == v else share for d in range(1, n_vec) if d != v)
        total += (whole_rows(0, c) if WHOLE[0] == v else 0) + whole_rows(v, c) + (2 * share if v else 0)
        blocks = next(n for n in range(1, n_vec + 1) if total % n == 0 and total // n <= rows)
        return shared.at[pl.ds(0, blocks), pl.ds(0, total // blocks)]

    def odd_moved(v, c):
        times = 2 if v == 0 else 0 if WHOLE[0] == v else 1
        return times and shared.at[0, pl.ds(0, times * halves(0, c)[1] * occ // 2)]

    if paired:
        for v in range(n_vec):
            for c in range(2):
                pl.when((me == v) & (chip == c))(functools.partial(sent, moved(v, c), v_send))
                if odd_moved(v, c):
                    pl.when((me == v) & (chip == c))(functools.partial(sent, odd_moved(v, c), odd_send))
        give().wait_send()
    else:
        sent(shared.at[pl.ds(0, others)], v_send)
    sent(pop.at[pl.ds(0, n_wlk - 1)], p_send)


def deliver(x_ref, log_ref, out_ref, outlog_ref, sem):
    copies = [
        pltpu.make_async_copy(log_ref.at[0:1], outlog_ref, sem.at[0]),
        pltpu.make_async_copy(x_ref, out_ref, sem.at[1]),
    ]
    for copy in copies:
        copy.start()
    for copy in copies:
        copy.wait()


def solution(mesh):
    n_vec, n_wlk = mesh.shape["vec"], mesh.shape["wlk"]

    def local(cholesky, orbitals, log_weights, parents, propagator):
        own, occ, basis = orbitals.shape
        assert own == 1 and n_wlk % 2 == 0
        vecs = cholesky.shape[0]
        share = vecs * occ // n_wlk
        assert share * n_wlk == vecs * occ
        paired = n_wlk == 4 and n_vec == 4 and vecs % (2 * FULL_PIECES) == 0
        pieces, walkers = 1, 2 if paired else 1
        others, chips = n_vec - 1, n_wlk // 2 - 1
        crossing = (1, 1) if paired else (others, chips)
        f32, bf16 = jnp.float32, jnp.bfloat16
        dma = pltpu.SemaphoreType.DMA
        regular = pltpu.SemaphoreType.REGULAR
        hbm = pl.BlockSpec(memory_space=pltpu.HBM)
        smem = pl.BlockSpec(memory_space=pltpu.SMEM)
        vmem = pl.BlockSpec(memory_space=pltpu.VMEM)
        x, logs = pl.pallas_call(
            functools.partial(kernel, n_vec, n_wlk, vecs, pieces, paired),
            out_shape=(pltpu.VMEM((occ, basis), f32), pltpu.VMEM((8, 128), f32)),
            in_specs=[hbm, hbm, smem, smem, hbm],
            out_specs=(vmem, vmem),
            scratch_shapes=[
                pltpu.VMEM((occ, basis), f32),
                pltpu.VMEM(propagator.shape, f32),
                pltpu.VMEM(propagator.shape, bf16),
                pltpu.VMEM((n_wlk, occ + EXTRA, basis), bf16),
                pltpu.VMEM((basis, walkers * occ), bf16),
                pltpu.VMEM((n_vec, vecs * occ, basis), bf16),
                pltpu.VMEM((walkers * occ, basis), f32),
                pltpu.VMEM((occ, basis), bf16),
                pltpu.VMEM((occ, basis), bf16),
                dma((3,)),
                dma((FULL_PIECES + 3, 1) if paired else (others, pieces)), dma(crossing + (pieces,)), dma((others,)), dma(crossing),
                dma((2 * chips + 1,)), dma, dma, dma, dma, dma, dma((FULL_PIECES,)),
                regular((others,)), regular((chips,)), regular,
            ],
            compiler_params=pltpu.CompilerParams(
                collective_id=0, has_side_effects=True, vmem_limit_bytes=60000000),
        )(
            cholesky.reshape(vecs * occ, basis),
            orbitals.reshape(occ, basis),
            log_weights,
            parents,
            propagator,
        )

        def here(array):
            return pltpu.with_memory_space_constraint(array, pltpu.VMEM)

        out, log = pl.pallas_call(
            deliver,
            out_shape=(
                jax.ShapeDtypeStruct((occ, basis), f32),
                jax.ShapeDtypeStruct((1, 128), f32),
            ),
            in_specs=[vmem, vmem],
            out_specs=(hbm, hbm),
            scratch_shapes=[dma((2,))],
        )(here(x), here(logs))
        return out.reshape(orbitals.shape), log[0, :1]

    placed = (
        P(("grp", "vec"), None, None),
        P(("grp", "vec", "wlk"), None, None),
        P(("grp", "vec", "wlk")),
        P(("grp", "vec", "wlk")),
        P("grp", None),
    )
    return jax.shard_map(
        local,
        mesh=mesh,
        in_specs=placed,
        out_specs=(P(("grp", "vec", "wlk"), None, None), P(("grp", "vec", "wlk"))),
        check_vma=False,
    )
```

```python
import functools
import math

import jax
import jax.numpy as jnp
from jax import lax
from jax.experimental import pallas as pl
from jax.experimental.pallas import tpu as pltpu
from jax.sharding import PartitionSpec as P

NS_ITERS = 2

gradient_step = 0.25
energy_step = 0.002
epsilon = 1e-06

MESH = pl.DeviceIdType.MESH
UNROLL_LIMIT = 8
EXTRA = 16
ORDER = ((3, 2, 1), (0, 3, 2), (0, 3, 1), (0, 1, 2))
WHOLE = tuple(order[-1] for order in ORDER)
BELOW = ((), ((0,),), ((0,),), ((0,), (2,), (1,)))
ABOVE = (((2,), (3,), (1,)), ((2, True, False), (3,)), ((3,),), ())
LATE = ((), ((2, False, True),), ((1,),), ())
FULL_PIECES = 3
MIXED = (False, False, True, False)


def dot(a, b):
    return lax.dot_general(a, b, (((1,), (0,)), ((), ())), preferred_element_type=jnp.float32)


def dot_t(a, b):
    return lax.dot_general(a, b, (((1,), (1,)), ((), ())), preferred_element_type=jnp.float32)


def each(count, body):
    if count <= UNROLL_LIMIT:
        for j in range(count):
            body(j)
    else:
        lax.fori_loop(0, count, lambda j, c: (body(j), c)[1], 0)


def kernel(
    n_vec, n_wlk, vecs, pieces, paired,
    chol_hbm, orb_hbm, logw, par, prop_hbm,
    out_ref, outlog_ref,
    orb, prop, propb, pop, turned, shared, acc, gsend, grecv,
    load_sem, z_recv, x_recv, near_recv, far_recv, p_recv, g_recv, v_send, p_send, g_send, last_recv,
    z_ready, x_ready, sib_ready,
):
    me = lax.axis_index("vec")
    mw = lax.axis_index("wlk")
    occ, basis = orb.shape
    rows = vecs * occ
    share = rows // n_wlk
    step = share // pieces
    n_chip = n_wlk // 2
    chip, core = lax.div(mw, 2), lax.rem(mw, 2)
    sibling = mw + 1 - 2 * core
    others, chips = n_vec - 1, n_chip - 1
    half = vecs // 2
    scale = 1.0 / math.sqrt(vecs * n_vec)

    def remote(src_ref, dst_ref, send, recv, where):
        return pltpu.make_async_remote_copy(
            src_ref=src_ref, dst_ref=dst_ref, send_sem=send, recv_sem=recv,
            device_id=where, device_id_type=MESH)

    def at(w, k):
        return pl.ds(pl.multiple_of(w * share + k * step, step), step)

    def quarter(w):
        return pl.ds(pl.multiple_of(w * share, share), share)

    def slot(src, dst):
        return jnp.where(src > dst, src - 1, src)

    def peer(i):
        return lax.rem(chip + 1 + i, n_chip) * 2 + core

    def source(j):
        if paired:
            first, *rest = (order[j] for order in ORDER)
            src = first
            for i, other in enumerate(rest):
                src = jnp.where(me == i + 1, other, src)
            return src
        lower = me - 1 - j
        return jnp.where(lower >= 0, lower, j + 1)

    def along(dst, k):
        return remote(chol_hbm.at[at(mw, k)], shared.at[me, at(mw, k)],
                      v_send, z_recv.at[slot(me, dst), k], {"vec": dst})

    def from_along(src, k):
        remote(shared.at[src, at(mw, k)], shared.at[src, at(mw, k)],
               v_send, z_recv.at[slot(src, me), k], {"wlk": sibling}).wait_recv()

    def across(src, i, k):
        return remote(shared.at[src, at(mw, k)], shared.at[src, at(mw, k)],
                      v_send, x_recv.at[slot(src, me), chips - 1 - i, k], {"wlk": peer(i)})

    def from_across(src, i, k):
        remote(shared.at[src, at(peer(i), k)], shared.at[src, at(peer(i), k)],
               v_send, x_recv.at[slot(src, me), i, k], {"wlk": sibling}).wait_recv()

    def beside(src, k):
        return remote(shared.at[src, at(mw, k)], shared.at[src, at(mw, k)],
                      v_send, near_recv.at[slot(src, me)], {"wlk": sibling})

    def from_beside(src):
        remote(shared.at[src, quarter(sibling)], shared.at[src, quarter(sibling)],
               v_send, near_recv.at[slot(src, me)], {"wlk": sibling}).wait_recv()

    def beyond(src, i, k):
        return remote(shared.at[src, at(peer(i), k)], shared.at[src, at(peer(i), k)],
                      v_send, far_recv.at[slot(src, me), i], {"wlk": sibling})

    def from_beyond(src, i):
        w = peer(i) + 1 - 2 * core
        remote(shared.at[src, quarter(w)], shared.at[src, quarter(w)],
               v_send, far_recv.at[slot(src, me), i], {"wlk": sibling}).wait_recv()

    def walker(w, index, where):
        return remote(pop.at[w], pop.at[w], p_send, p_recv.at[index], {"wlk": where})

    load_orb = pltpu.make_async_copy(orb_hbm, orb, load_sem.at[0])
    load_own = pltpu.make_async_copy(chol_hbm, shared.at[me], load_sem.at[1])
    load_prop = pltpu.make_async_copy(prop_hbm, prop, load_sem.at[2])

    barrier = pltpu.get_barrier_semaphore()

    def greet(semaphore, where):
        pl.semaphore_signal(semaphore, inc=1, device_id=where, device_id_type=MESH)

    each(others, lambda j: pl.when(j + 1 > me)(lambda: greet(barrier, {"vec": j + 1})))
    each(chips, lambda j: pl.when(j + 1 > chip)(
        lambda: greet(barrier, {"wlk": (j + 1) * 2 + core})))
    pl.when(core == 0)(lambda: greet(barrier, {"wlk": sibling}))

    load_orb.start()
    before = me + chip + core
    pl.when(before > 0)(lambda: pl.semaphore_wait(barrier, before))

    each(others, lambda j: pl.when(j < me)(lambda: greet(z_ready.at[me - 1], {"vec": j})))
    each(chips, lambda j: pl.when(j < chip)(
        lambda: greet(x_ready.at[chip - 1], {"wlk": j * 2 + core})))
    pl.when(core == 1)(lambda: greet(sib_ready, {"wlk": sibling}))

    def send_along(dst):
        for k in range(pieces):
            along(dst, k).start()

    def send_up(j):
        @pl.when(me + j + 1 < n_vec)
        def _():
            pl.semaphore_wait(z_ready.at[me + j], 1)
            send_along(me + j + 1)

    batch = vecs // FULL_PIECES
    alone = (FULL_PIECES - 1) * batch

    def whole_parts(v):
        parts = [(k * batch, batch) for k in range(FULL_PIECES)]
        return parts[:-1] + [(alone + 1, batch - 1)] if MIXED[v] else parts

    def core_rows(c, begin, count):
        part = count * occ // 2
        return pl.ds(pl.multiple_of(begin * occ + c * part, part), part)

    def to_core(src, dst, begin, count, k):
        remote(chol_hbm.at[core_rows(core, begin, count)], shared.at[src, core_rows(core, begin, count)],
               v_send, z_recv.at[2 + k, 0], {"vec": dst}).start()

    def send(src, dst, some=True, rest=True):
        if dst > src and some:
            pl.semaphore_wait(z_ready.at[dst - 1], 1)
        if WHOLE[dst] == src:
            if some and MIXED[dst]:
                pl.when(chip == 0)(lambda: to_core(src, dst, alone, 1, FULL_PIECES))
            for k, part in enumerate(whole_parts(dst) if rest else ()):
                to_core(src, dst, *part, k)
        else:
            remote(chol_hbm.at[quarter(mw)], shared.at[src, quarter(mw)],
                   v_send, z_recv.at[ORDER[dst].index(src), 0], {"vec": dst}).start()

    def send_all(plan):
        for v in range(n_vec):
            @pl.when(me == v)
            def _():
                for d in plan[v]:
                    send(v, *d)

    if paired:
        send_all(BELOW)
    else:
        each(others, lambda j: pl.when(j < me)(lambda: send_along(j)))
    load_own.start()
    load_prop.start()

    load_orb.wait()
    pop[mw, 0:occ] = orb[...].astype(jnp.bfloat16)
    whole = jnp.full((EXTRA, basis), logw[0], jnp.float32)
    high = whole.astype(jnp.bfloat16).astype(jnp.float32)
    middle = (whole - high).astype(jnp.bfloat16).astype(jnp.float32)
    low = whole - high - middle
    lane = lax.broadcasted_iota(jnp.int32, (EXTRA, basis), 1)
    parent = jnp.full((EXTRA, basis), par[0], jnp.int32).astype(jnp.float32)
    pop[mw, occ:occ + EXTRA] = jnp.where(
        lane == 0, high, jnp.where(lane == 1, middle, jnp.where(
            lane == 2, low, jnp.where(lane == 3, parent, 0.0)))).astype(jnp.bfloat16)

    pl.when(core == 0)(lambda: pl.semaphore_wait(sib_ready, 1))
    walker(mw, 2 * chips, sibling).start()
    if paired:
        pl.when(chip == 1)(lambda: walker(mw, 0, peer(0)).start())
        send_all([d[:1] for d in ABOVE])

        @pl.when(chip == 0)
        def _():
            pl.semaphore_wait(x_ready.at[0], 1)
            walker(mw, 0, peer(0)).start()

        send_all([d[1:] for d in ABOVE])
    else:
        each(chips, lambda j: pl.when(j + 1 > chip)(lambda: pl.semaphore_wait(x_ready.at[j], 1)))
        for i in range(chips):
            walker(mw, chips - 1 - i, peer(i)).start()
        each(others, send_up)

    def take(j, k):
        src = source(j)
        from_along(src, k)
        for i in range(chips):
            across(src, i, k).start()
        beside(src, k).start()

    def pass_on(j, k):
        src = source(j)
        for i in range(chips):
            from_across(src, i, k)
            beyond(src, i, k).start()

    def pass_walkers():
        for i in range(chips):
            walker(peer(i), i, sibling).wait_recv()
            walker(peer(i), chips + i, sibling).start()

    def all_walkers():
        for i in range(chips + 1):
            w = peer(i) + 1 - 2 * core
            walker(w, chips + i, sibling).wait_recv()

    row = lax.broadcasted_iota(jnp.int32, (occ, occ), 0)
    col = lax.broadcasted_iota(jnp.int32, (occ, occ), 1)
    diagonal = row == col

    def work(src, first, count):
        vectors = shared[src, pl.ds(pl.multiple_of(first * occ, occ), count * occ)]
        s = dot(vectors, turned[:, 0:occ])
        swapped = (-scale * s).astype(jnp.bfloat16)
        blocks = [swapped[g * occ:(g + 1) * occ, :] for g in range(count)]
        direct = jnp.zeros((occ, basis), jnp.float32)
        for g in range(count):
            on_diagonal = jnp.where(diagonal, s[g * occ:(g + 1) * occ, :], 0.0)
            tg = jnp.sum(jnp.sum(on_diagonal, axis=0, keepdims=True), axis=1, keepdims=True)
            direct += (scale * tg) * vectors[g * occ:(g + 1) * occ].astype(jnp.float32)
        adjoint = jnp.concatenate(blocks, axis=1) if count > 1 else blocks[0]
        acc[0:occ] += dot(adjoint, vectors) + direct

    def pick(w):
        parent = jnp.broadcast_to(pop[w, occ:occ + 1, 3:4].astype(jnp.float32), (occ + EXTRA, basis))
        picked = pop[0].astype(jnp.float32)
        for m in range(1, n_wlk):
            picked = jnp.where(parent == m, pop[m].astype(jnp.float32), picked)
        return picked

    def choose():
        picked = pick(mw)
        orb[...] = picked[0:occ]
        logs = picked[occ:occ + 8, 0:128]
        logs = jnp.where(lax.broadcasted_iota(jnp.int32, (8, 128), 1) < 3, logs, 0.0)
        outlog_ref[...] = jnp.broadcast_to(jnp.sum(logs, axis=1, keepdims=True), (8, 128))
        chosen = picked[0:occ]
        if paired:
            chosen = jnp.concatenate([chosen, pick(peer(0))[0:occ]], axis=0)
        turned[...] = chosen.T.astype(jnp.bfloat16)
        acc[...] = jnp.zeros_like(acc)

    def turn_propagator():
        load_prop.wait()
        propb[...] = prop[...].T.astype(jnp.bfloat16)

    where = lax.broadcasted_iota(jnp.int32, (occ, 2 * occ), 1)
    left = where < occ
    pair_diagonal = lax.broadcasted_iota(jnp.int32, (occ, 2 * occ), 0) == jnp.where(
        left, where, where - occ)

    def work_pair(src, begin, count, last):
        vectors = shared[src, pl.ds(pl.multiple_of(begin * occ, occ), count * occ)]
        s = dot(vectors, turned[...])
        swapped = (-scale * s).astype(jnp.bfloat16)
        blocks = [swapped[g * occ:(g + 1) * occ, :] for g in range(count)]
        direct = [jnp.zeros((occ, basis), jnp.float32)] * 2
        for g in range(count):
            sg = s[g * occ:(g + 1) * occ, :]
            along_diagonal = jnp.sum(jnp.where(pair_diagonal, sg, 0.0), axis=0, keepdims=True)
            block = vectors[g * occ:(g + 1) * occ].astype(jnp.float32)
            for i in range(2):
                side = jnp.where(left[0:1] if i == 0 else jnp.logical_not(left[0:1]), along_diagonal, 0.0)
                direct[i] = direct[i] + scale * jnp.sum(side, axis=1, keepdims=True) * block
        mine = jnp.concatenate([b[:, 0:occ] for b in blocks], axis=1)
        theirs = jnp.concatenate([b[:, occ:] for b in blocks], axis=1)
        if last:
            gsend[...] = (acc[occ:] + dot(theirs, vectors) + direct[1]).astype(jnp.bfloat16)
            give().start()
            acc[0:occ] += dot(mine, vectors) + direct[0]
        else:
            acc[...] += dot(jnp.concatenate([mine, theirs], axis=0), vectors) + jnp.concatenate(
                direct, axis=0)

    def gather(v):
        first, second, final = ORDER[v]

        def landed(view, signal):
            remote(view, view, v_send, signal, {"wlk": sibling}).wait_recv()

        def pass_beside(view, signal):
            remote(view, view, v_send, signal, {"wlk": sibling}).start()

        def take(src):
            view = shared.at[src, quarter(mw)]
            landed(view, z_recv.at[ORDER[v].index(src), 0])
            pass_beside(view, near_recv.at[src - (src > v)])

        def finish(src, last):
            landed(shared.at[src, quarter(sibling)], near_recv.at[src - (src > v)])
            work_pair(src, chip * half, half, last)

        at_final = final - (final > v)
        take(first)
        take(second)
        finish(first, False)

        def lone():
            finish(second, False)
            view = shared.at[final, core_rows(core, alone, 1)]
            landed(view, z_recv.at[2 + FULL_PIECES, 0])
            pass_beside(view, near_recv.at[at_final])
            landed(shared.at[final, core_rows(1 - core, alone, 1)], near_recv.at[at_final])
            work_pair(final, alone, 1, True)

        if MIXED[v]:
            pl.when(chip == 0)(lone)
            pl.when(chip == 1)(lambda: finish(second, True))
        else:
            finish(second, True)
        parts = whole_parts(v)
        for k in range(FULL_PIECES + 1):
            if k < FULL_PIECES:
                view = shared.at[final, core_rows(core, *parts[k])]
                landed(view, z_recv.at[2 + k, 0])
                pass_beside(view, last_recv.at[k])
            if k > 0:
                landed(shared.at[final, core_rows(1 - core, *parts[k - 1])], last_recv.at[k - 1])
                work(final, *parts[k - 1])

    def give():
        return remote(gsend, grecv, g_send, g_recv, {"wlk": peer(0)})

    if paired:
        pass_walkers()
        send_all(LATE)
        turn_propagator()
        all_walkers()
        choose()
        load_own.wait()
        work_pair(me, chip * half, half, False)
        for v in range(n_vec):
            pl.when(me == v)(functools.partial(gather, v))
        give().wait_recv()
        acc[0:occ] += grecv[...].astype(jnp.float32)
    else:
        pass_walkers()
        turn_propagator()
        all_walkers()
        choose()
        load_own.wait()
        work(me, 0, vecs)

        def one(j):
            for k in range(pieces):
                take(j, k)
            for k in range(pieces):
                pass_on(j, k)
            from_beside(source(j))
            for i in range(chips):
                from_beyond(source(j), i)
            work(source(j), 0, vecs)

        each(others, one)

    theta = orb[...]
    gradient = acc[0:occ]
    energy = 0.5 * jnp.sum(jnp.sum(theta * gradient, axis=0, keepdims=True), axis=1, keepdims=True)
    outlog_ref[...] -= energy_step * jnp.broadcast_to(energy, (8, 128))
    stepped = theta - gradient_step * gradient
    x = dot(stepped.astype(jnp.bfloat16), propb[...])
    mean_square = jnp.sum(jnp.sum(x * x, axis=0, keepdims=True), axis=1, keepdims=True)
    mean_square = mean_square / (occ * basis)
    norm = 1.0 / jnp.sqrt(mean_square + epsilon)
    for it in range(NS_ITERS):
        xb = x.astype(jnp.bfloat16)
        inter = dot_t(xb, xb) * (norm * norm / basis if it == 0 else 1.0 / basis)
        x = 0.5 * (3.0 * x - dot(inter.astype(jnp.bfloat16), xb))
        if it == 0:
            x = norm * x
    out_ref[...] = x

    def sent(view, semaphore):
        remote(view, view, semaphore, semaphore, {"wlk": sibling}).wait_send()

    def whole_rows(v, c):
        return (rows - (occ if MIXED[v] and c else 0)) // 2

    def moved(v, c):
        total = sum(whole_rows(d, c) if WHOLE[d] == v else share for d in range(n_vec) if d != v)
        total += whole_rows(v, c) + 2 * share
        blocks = next(n for n in range(1, n_vec + 1) if total % n == 0 and total // n <= rows)
        return shared.at[pl.ds(0, blocks), pl.ds(0, total // blocks)]

    if paired:
        for v in range(n_vec):
            for c in range(2):
                pl.when((me == v) & (chip == c))(functools.partial(sent, moved(v, c), v_send))
        give().wait_send()
    else:
        sent(shared.at[pl.ds(0, others)], v_send)
    sent(pop.at[pl.ds(0, n_wlk - 1)], p_send)


def deliver(x_ref, log_ref, out_ref, outlog_ref, sem):
    copies = [
        pltpu.make_async_copy(log_ref.at[0:1], outlog_ref, sem.at[0]),
        pltpu.make_async_copy(x_ref, out_ref, sem.at[1]),
    ]
    for copy in copies:
        copy.start()
    for copy in copies:
        copy.wait()


def solution(mesh):
    n_vec, n_wlk = mesh.shape["vec"], mesh.shape["wlk"]

    def local(cholesky, orbitals, log_weights, parents, propagator):
        own, occ, basis = orbitals.shape
        assert own == 1 and n_wlk % 2 == 0
        vecs = cholesky.shape[0]
        share = vecs * occ // n_wlk
        assert share * n_wlk == vecs * occ
        paired = n_wlk == 4 and n_vec == 4 and vecs % (2 * FULL_PIECES) == 0
        pieces, walkers = 1, 2 if paired else 1
        others, chips = n_vec - 1, n_wlk // 2 - 1
        crossing = (1, 1) if paired else (others, chips)
        f32, bf16 = jnp.float32, jnp.bfloat16
        dma = pltpu.SemaphoreType.DMA
        regular = pltpu.SemaphoreType.REGULAR
        hbm = pl.BlockSpec(memory_space=pltpu.HBM)
        smem = pl.BlockSpec(memory_space=pltpu.SMEM)
        vmem = pl.BlockSpec(memory_space=pltpu.VMEM)
        x, logs = pl.pallas_call(
            functools.partial(kernel, n_vec, n_wlk, vecs, pieces, paired),
            out_shape=(pltpu.VMEM((occ, basis), f32), pltpu.VMEM((8, 128), f32)),
            in_specs=[hbm, hbm, smem, smem, hbm],
            out_specs=(vmem, vmem),
            scratch_shapes=[
                pltpu.VMEM((occ, basis), f32),
                pltpu.VMEM(propagator.shape, f32),
                pltpu.VMEM(propagator.shape, bf16),
                pltpu.VMEM((n_wlk, occ + EXTRA, basis), bf16),
                pltpu.VMEM((basis, walkers * occ), bf16),
                pltpu.VMEM((n_vec, vecs * occ, basis), bf16),
                pltpu.VMEM((walkers * occ, basis), f32),
                pltpu.VMEM((occ, basis), bf16),
                pltpu.VMEM((occ, basis), bf16),
                dma((3,)),
                dma((FULL_PIECES + 3, 1) if paired else (others, pieces)), dma(crossing + (pieces,)), dma((others,)), dma(crossing),
                dma((2 * chips + 1,)), dma, dma, dma, dma, dma((FULL_PIECES,)),
                regular((others,)), regular((chips,)), regular,
            ],
            compiler_params=pltpu.CompilerParams(
                collective_id=0, has_side_effects=True, vmem_limit_bytes=60000000),
        )(
            cholesky.reshape(vecs * occ, basis),
            orbitals.reshape(occ, basis),
            log_weights,
            parents,
            propagator,
        )

        def here(array):
            return pltpu.with_memory_space_constraint(array, pltpu.VMEM)

        out, log = pl.pallas_call(
            deliver,
            out_shape=(
                jax.ShapeDtypeStruct((occ, basis), f32),
                jax.ShapeDtypeStruct((1, 128), f32),
            ),
            in_specs=[vmem, vmem],
            out_specs=(hbm, hbm),
            scratch_shapes=[dma((2,))],
        )(here(x), here(logs))
        return out.reshape(orbitals.shape), log[0, :1]

    placed = (
        P(("grp", "vec"), None, None),
        P(("grp", "vec", "wlk"), None, None),
        P(("grp", "vec", "wlk")),
        P(("grp", "vec", "wlk")),
        P("grp", None),
    )
    return jax.shard_map(
        local,
        mesh=mesh,
        in_specs=placed,
        out_specs=(P(("grp", "vec", "wlk"), None, None), P(("grp", "vec", "wlk"))),
        check_vma=False,
    )
```

```python
import functools
import math

import jax
import jax.numpy as jnp
from jax import lax
from jax.experimental import pallas as pl
from jax.experimental.pallas import tpu as pltpu
from jax.sharding import PartitionSpec as P

NS_ITERS = 2

gradient_step = 0.25
energy_step = 0.002
epsilon = 1e-06

MESH = pl.DeviceIdType.MESH
UNROLL_LIMIT = 8
EXTRA = 16
ORDER = ((3, 2, 1), (0, 3, 2), (0, 3, 1), (0, 1, 2))
WHOLE = tuple(order[-1] for order in ORDER)
BELOW = ((), ((0,),), ((0,),), ((0,), (2,), (1,)))
ABOVE = (((2,), (3,), (1,)), ((2, True, False), (3,)), ((3,),), ())
LATE = ((), ((2, False, True),), ((1,),), ())
FULL_PIECES = 3
MIXED = (False, False, True, False)


def dot(a, b):
    return lax.dot_general(a, b, (((1,), (0,)), ((), ())), preferred_element_type=jnp.float32)


def dot_t(a, b):
    return lax.dot_general(a, b, (((1,), (1,)), ((), ())), preferred_element_type=jnp.float32)


def each(count, body):
    if count <= UNROLL_LIMIT:
        for j in range(count):
            body(j)
    else:
        lax.fori_loop(0, count, lambda j, c: (body(j), c)[1], 0)


def kernel(
    n_vec, n_wlk, vecs, pieces, paired,
    chol_hbm, orb_hbm, logw, par, prop_hbm,
    out_ref, outlog_ref,
    orb, prop, propb, pop, turned, shared, acc, gsend, grecv,
    load_sem, z_recv, x_recv, near_recv, far_recv, p_recv, g_recv, v_send, p_send, g_send, last_recv,
    z_ready, x_ready, sib_ready,
):
    me = lax.axis_index("vec")
    mw = lax.axis_index("wlk")
    occ, basis = orb.shape
    rows = vecs * occ
    share = rows // n_wlk
    step = share // pieces
    n_chip = n_wlk // 2
    chip, core = lax.div(mw, 2), lax.rem(mw, 2)
    sibling = mw + 1 - 2 * core
    others, chips = n_vec - 1, n_chip - 1
    half = vecs // 2
    scale = 1.0 / math.sqrt(vecs * n_vec)

    def remote(src_ref, dst_ref, send, recv, where):
        return pltpu.make_async_remote_copy(
            src_ref=src_ref, dst_ref=dst_ref, send_sem=send, recv_sem=recv,
            device_id=where, device_id_type=MESH)

    def at(w, k):
        return pl.ds(pl.multiple_of(w * share + k * step, step), step)

    def quarter(w):
        return pl.ds(pl.multiple_of(w * share, share), share)

    def slot(src, dst):
        return jnp.where(src > dst, src - 1, src)

    def peer(i):
        return lax.rem(chip + 1 + i, n_chip) * 2 + core

    def source(j):
        if paired:
            first, *rest = (order[j] for order in ORDER)
            src = first
            for i, other in enumerate(rest):
                src = jnp.where(me == i + 1, other, src)
            return src
        lower = me - 1 - j
        return jnp.where(lower >= 0, lower, j + 1)

    def along(dst, k):
        return remote(chol_hbm.at[at(mw, k)], shared.at[me, at(mw, k)],
                      v_send, z_recv.at[slot(me, dst), k], {"vec": dst})

    def from_along(src, k):
        remote(shared.at[src, at(mw, k)], shared.at[src, at(mw, k)],
               v_send, z_recv.at[slot(src, me), k], {"wlk": sibling}).wait_recv()

    def across(src, i, k):
        return remote(shared.at[src, at(mw, k)], shared.at[src, at(mw, k)],
                      v_send, x_recv.at[slot(src, me), chips - 1 - i, k], {"wlk": peer(i)})

    def from_across(src, i, k):
        remote(shared.at[src, at(peer(i), k)], shared.at[src, at(peer(i), k)],
               v_send, x_recv.at[slot(src, me), i, k], {"wlk": sibling}).wait_recv()

    def beside(src, k):
        return remote(shared.at[src, at(mw, k)], shared.at[src, at(mw, k)],
                      v_send, near_recv.at[slot(src, me)], {"wlk": sibling})

    def from_beside(src):
        remote(shared.at[src, quarter(sibling)], shared.at[src, quarter(sibling)],
               v_send, near_recv.at[slot(src, me)], {"wlk": sibling}).wait_recv()

    def beyond(src, i, k):
        return remote(shared.at[src, at(peer(i), k)], shared.at[src, at(peer(i), k)],
                      v_send, far_recv.at[slot(src, me), i], {"wlk": sibling})

    def from_beyond(src, i):
        w = peer(i) + 1 - 2 * core
        remote(shared.at[src, quarter(w)], shared.at[src, quarter(w)],
               v_send, far_recv.at[slot(src, me), i], {"wlk": sibling}).wait_recv()

    def walker(w, index, where):
        return remote(pop.at[w], pop.at[w], p_send, p_recv.at[index], {"wlk": where})

    load_orb = pltpu.make_async_copy(orb_hbm, orb, load_sem.at[0])
    load_own = pltpu.make_async_copy(chol_hbm, shared.at[me], load_sem.at[1])
    load_prop = pltpu.make_async_copy(prop_hbm, prop, load_sem.at[2])

    barrier = pltpu.get_barrier_semaphore()

    def greet(semaphore, where):
        pl.semaphore_signal(semaphore, inc=1, device_id=where, device_id_type=MESH)

    each(others, lambda j: pl.when(j + 1 > me)(lambda: greet(barrier, {"vec": j + 1})))
    each(chips, lambda j: pl.when(j + 1 > chip)(
        lambda: greet(barrier, {"wlk": (j + 1) * 2 + core})))
    pl.when(core == 0)(lambda: greet(barrier, {"wlk": sibling}))

    load_orb.start()
    before = me + chip + core
    pl.when(before > 0)(lambda: pl.semaphore_wait(barrier, before))

    def send_along(dst):
        for k in range(pieces):
            along(dst, k).start()

    def send_up(j):
        @pl.when(me + j + 1 < n_vec)
        def _():
            pl.semaphore_wait(z_ready.at[me + j], 1)
            send_along(me + j + 1)

    batch = vecs // FULL_PIECES
    alone = (FULL_PIECES - 1) * batch

    def whole_parts(v):
        parts = [(k * batch, batch) for k in range(FULL_PIECES)]
        return parts[:-1] + [(alone + 1, batch - 1)] if MIXED[v] else parts

    def core_rows(c, begin, count):
        part = count * occ // 2
        return pl.ds(pl.multiple_of(begin * occ + c * part, part), part)

    def to_core(src, dst, begin, count, k):
        remote(chol_hbm.at[core_rows(core, begin, count)], shared.at[src, core_rows(core, begin, count)],
               v_send, z_recv.at[2 + k, 0], {"vec": dst}).start()

    def send(src, dst, some=True, rest=True):
        if dst > src and some:
            pl.semaphore_wait(z_ready.at[dst - 1], 1)
        if WHOLE[dst] == src:
            if some and MIXED[dst]:
                pl.when(chip == 0)(lambda: to_core(src, dst, alone, 1, FULL_PIECES))
            for k, part in enumerate(whole_parts(dst) if rest else ()):
                to_core(src, dst, *part, k)
        else:
            remote(chol_hbm.at[quarter(mw)], shared.at[src, quarter(mw)],
                   v_send, z_recv.at[ORDER[dst].index(src), 0], {"vec": dst}).start()

    def send_all(plan):
        for v in range(n_vec):
            @pl.when(me == v)
            def _():
                for d in plan[v]:
                    send(v, *d)

    if paired:
        send_all(BELOW)
    else:
        each(others, lambda j: pl.when(j < me)(lambda: send_along(j)))
    each(others, lambda j: pl.when(j < me)(lambda: greet(z_ready.at[me - 1], {"vec": j})))
    each(chips, lambda j: pl.when(j < chip)(
        lambda: greet(x_ready.at[chip - 1], {"wlk": j * 2 + core})))
    pl.when(core == 1)(lambda: greet(sib_ready, {"wlk": sibling}))

    load_own.start()
    load_prop.start()

    load_orb.wait()
    pop[mw, 0:occ] = orb[...].astype(jnp.bfloat16)
    whole = jnp.full((EXTRA, basis), logw[0], jnp.float32)
    high = whole.astype(jnp.bfloat16).astype(jnp.float32)
    middle = (whole - high).astype(jnp.bfloat16).astype(jnp.float32)
    low = whole - high - middle
    lane = lax.broadcasted_iota(jnp.int32, (EXTRA, basis), 1)
    parent = jnp.full((EXTRA, basis), par[0], jnp.int32).astype(jnp.float32)
    pop[mw, occ:occ + EXTRA] = jnp.where(
        lane == 0, high, jnp.where(lane == 1, middle, jnp.where(
            lane == 2, low, jnp.where(lane == 3, parent, 0.0)))).astype(jnp.bfloat16)

    pl.when(core == 0)(lambda: pl.semaphore_wait(sib_ready, 1))
    walker(mw, 2 * chips, sibling).start()
    if paired:
        pl.when(chip == 1)(lambda: walker(mw, 0, peer(0)).start())
        send_all([d[:1] for d in ABOVE])

        @pl.when(chip == 0)
        def _():
            pl.semaphore_wait(x_ready.at[0], 1)
            walker(mw, 0, peer(0)).start()

        send_all([d[1:] for d in ABOVE])
    else:
        each(chips, lambda j: pl.when(j + 1 > chip)(lambda: pl.semaphore_wait(x_ready.at[j], 1)))
        for i in range(chips):
            walker(mw, chips - 1 - i, peer(i)).start()
        each(others, send_up)

    def take(j, k):
        src = source(j)
        from_along(src, k)
        for i in range(chips):
            across(src, i, k).start()
        beside(src, k).start()

    def pass_on(j, k):
        src = source(j)
        for i in range(chips):
            from_across(src, i, k)
            beyond(src, i, k).start()

    def pass_walkers():
        for i in range(chips):
            walker(peer(i), i, sibling).wait_recv()
            walker(peer(i), chips + i, sibling).start()

    def all_walkers():
        for i in range(chips + 1):
            w = peer(i) + 1 - 2 * core
            walker(w, chips + i, sibling).wait_recv()

    row = lax.broadcasted_iota(jnp.int32, (occ, occ), 0)
    col = lax.broadcasted_iota(jnp.int32, (occ, occ), 1)
    diagonal = row == col

    def work(src, first, count):
        vectors = shared[src, pl.ds(pl.multiple_of(first * occ, occ), count * occ)]
        s = dot(vectors, turned[:, 0:occ])
        swapped = (-scale * s).astype(jnp.bfloat16)
        blocks = [swapped[g * occ:(g + 1) * occ, :] for g in range(count)]
        direct = jnp.zeros((occ, basis), jnp.float32)
        for g in range(count):
            on_diagonal = jnp.where(diagonal, s[g * occ:(g + 1) * occ, :], 0.0)
            tg = jnp.sum(jnp.sum(on_diagonal, axis=0, keepdims=True), axis=1, keepdims=True)
            direct += (scale * tg) * vectors[g * occ:(g + 1) * occ].astype(jnp.float32)
        adjoint = jnp.concatenate(blocks, axis=1) if count > 1 else blocks[0]
        acc[0:occ] += dot(adjoint, vectors) + direct

    def pick(w):
        parent = jnp.broadcast_to(pop[w, occ:occ + 1, 3:4].astype(jnp.float32), (occ + EXTRA, basis))
        picked = pop[0].astype(jnp.float32)
        for m in range(1, n_wlk):
            picked = jnp.where(parent == m, pop[m].astype(jnp.float32), picked)
        return picked

    def choose():
        picked = pick(mw)
        orb[...] = picked[0:occ]
        logs = picked[occ:occ + 8, 0:128]
        logs = jnp.where(lax.broadcasted_iota(jnp.int32, (8, 128), 1) < 3, logs, 0.0)
        outlog_ref[...] = jnp.broadcast_to(jnp.sum(logs, axis=1, keepdims=True), (8, 128))
        chosen = picked[0:occ]
        if paired:
            chosen = jnp.concatenate([chosen, pick(peer(0))[0:occ]], axis=0)
        turned[...] = chosen.T.astype(jnp.bfloat16)
        acc[...] = jnp.zeros_like(acc)

    def turn_propagator():
        load_prop.wait()
        propb[...] = prop[...].T.astype(jnp.bfloat16)

    where = lax.broadcasted_iota(jnp.int32, (occ, 2 * occ), 1)
    left = where < occ
    pair_diagonal = lax.broadcasted_iota(jnp.int32, (occ, 2 * occ), 0) == jnp.where(
        left, where, where - occ)

    def work_pair(src, begin, count, last):
        vectors = shared[src, pl.ds(pl.multiple_of(begin * occ, occ), count * occ)]
        s = dot(vectors, turned[...])
        swapped = (-scale * s).astype(jnp.bfloat16)
        blocks = [swapped[g * occ:(g + 1) * occ, :] for g in range(count)]
        direct = [jnp.zeros((occ, basis), jnp.float32)] * 2
        for g in range(count):
            sg = s[g * occ:(g + 1) * occ, :]
            along_diagonal = jnp.sum(jnp.where(pair_diagonal, sg, 0.0), axis=0, keepdims=True)
            block = vectors[g * occ:(g + 1) * occ].astype(jnp.float32)
            for i in range(2):
                side = jnp.where(left[0:1] if i == 0 else jnp.logical_not(left[0:1]), along_diagonal, 0.0)
                direct[i] = direct[i] + scale * jnp.sum(side, axis=1, keepdims=True) * block
        mine = jnp.concatenate([b[:, 0:occ] for b in blocks], axis=1)
        theirs = jnp.concatenate([b[:, occ:] for b in blocks], axis=1)
        if last:
            gsend[...] = (acc[occ:] + dot(theirs, vectors) + direct[1]).astype(jnp.bfloat16)
            give().start()
            acc[0:occ] += dot(mine, vectors) + direct[0]
        else:
            acc[...] += dot(jnp.concatenate([mine, theirs], axis=0), vectors) + jnp.concatenate(
                direct, axis=0)

    def gather(v):
        first, second, final = ORDER[v]

        def landed(view, signal):
            remote(view, view, v_send, signal, {"wlk": sibling}).wait_recv()

        def pass_beside(view, signal):
            remote(view, view, v_send, signal, {"wlk": sibling}).start()

        def take(src):
            view = shared.at[src, quarter(mw)]
            landed(view, z_recv.at[ORDER[v].index(src), 0])
            pass_beside(view, near_recv.at[src - (src > v)])

        def finish(src, last):
            landed(shared.at[src, quarter(sibling)], near_recv.at[src - (src > v)])
            work_pair(src, chip * half, half, last)

        at_final = final - (final > v)
        take(first)
        take(second)
        finish(first, False)

        def lone():
            finish(second, False)
            view = shared.at[final, core_rows(core, alone, 1)]
            landed(view, z_recv.at[2 + FULL_PIECES, 0])
            pass_beside(view, near_recv.at[at_final])
            landed(shared.at[final, core_rows(1 - core, alone, 1)], near_recv.at[at_final])
            work_pair(final, alone, 1, True)

        if MIXED[v]:
            pl.when(chip == 0)(lone)
            pl.when(chip == 1)(lambda: finish(second, True))
        else:
            finish(second, True)
        parts = whole_parts(v)
        for k in range(FULL_PIECES + 1):
            if k < FULL_PIECES:
                view = shared.at[final, core_rows(core, *parts[k])]
                landed(view, z_recv.at[2 + k, 0])
                pass_beside(view, last_recv.at[k])
            if k > 0:
                landed(shared.at[final, core_rows(1 - core, *parts[k - 1])], last_recv.at[k - 1])
                work(final, *parts[k - 1])

    def give():
        return remote(gsend, grecv, g_send, g_recv, {"wlk": peer(0)})

    if paired:
        pass_walkers()
        send_all(LATE)
        turn_propagator()
        all_walkers()
        choose()
        load_own.wait()
        work_pair(me, chip * half, half, False)
        for v in range(n_vec):
            pl.when(me == v)(functools.partial(gather, v))
        give().wait_recv()
        acc[0:occ] += grecv[...].astype(jnp.float32)
    else:
        pass_walkers()
        turn_propagator()
        all_walkers()
        choose()
        load_own.wait()
        work(me, 0, vecs)

        def one(j):
            for k in range(pieces):
                take(j, k)
            for k in range(pieces):
                pass_on(j, k)
            from_beside(source(j))
            for i in range(chips):
                from_beyond(source(j), i)
            work(source(j), 0, vecs)

        each(others, one)

    theta = orb[...]
    gradient = acc[0:occ]
    energy = 0.5 * jnp.sum(jnp.sum(theta * gradient, axis=0, keepdims=True), axis=1, keepdims=True)
    outlog_ref[...] -= energy_step * jnp.broadcast_to(energy, (8, 128))
    stepped = theta - gradient_step * gradient
    x = dot(stepped.astype(jnp.bfloat16), propb[...])
    mean_square = jnp.sum(jnp.sum(x * x, axis=0, keepdims=True), axis=1, keepdims=True)
    mean_square = mean_square / (occ * basis)
    norm = 1.0 / jnp.sqrt(mean_square + epsilon)
    for it in range(NS_ITERS):
        xb = x.astype(jnp.bfloat16)
        inter = dot_t(xb, xb) * (norm * norm / basis if it == 0 else 1.0 / basis)
        x = 0.5 * (3.0 * x - dot(inter.astype(jnp.bfloat16), xb))
        if it == 0:
            x = norm * x
    out_ref[...] = x

    def sent(view, semaphore):
        remote(view, view, semaphore, semaphore, {"wlk": sibling}).wait_send()

    def whole_rows(v, c):
        return (rows - (occ if MIXED[v] and c else 0)) // 2

    def moved(v, c):
        total = sum(whole_rows(d, c) if WHOLE[d] == v else share for d in range(n_vec) if d != v)
        total += whole_rows(v, c) + 2 * share
        blocks = next(n for n in range(1, n_vec + 1) if total % n == 0 and total // n <= rows)
        return shared.at[pl.ds(0, blocks), pl.ds(0, total // blocks)]

    if paired:
        for v in range(n_vec):
            for c in range(2):
                pl.when((me == v) & (chip == c))(functools.partial(sent, moved(v, c), v_send))
        give().wait_send()
    else:
        sent(shared.at[pl.ds(0, others)], v_send)
    sent(pop.at[pl.ds(0, n_wlk - 1)], p_send)


def deliver(x_ref, log_ref, out_ref, outlog_ref, sem):
    copies = [
        pltpu.make_async_copy(log_ref.at[0:1], outlog_ref, sem.at[0]),
        pltpu.make_async_copy(x_ref, out_ref, sem.at[1]),
    ]
    for copy in copies:
        copy.start()
    for copy in copies:
        copy.wait()


def solution(mesh):
    n_vec, n_wlk = mesh.shape["vec"], mesh.shape["wlk"]

    def local(cholesky, orbitals, log_weights, parents, propagator):
        own, occ, basis = orbitals.shape
        assert own == 1 and n_wlk % 2 == 0
        vecs = cholesky.shape[0]
        share = vecs * occ // n_wlk
        assert share * n_wlk == vecs * occ
        paired = n_wlk == 4 and n_vec == 4 and vecs % (2 * FULL_PIECES) == 0
        pieces, walkers = 1, 2 if paired else 1
        others, chips = n_vec - 1, n_wlk // 2 - 1
        crossing = (1, 1) if paired else (others, chips)
        f32, bf16 = jnp.float32, jnp.bfloat16
        dma = pltpu.SemaphoreType.DMA
        regular = pltpu.SemaphoreType.REGULAR
        hbm = pl.BlockSpec(memory_space=pltpu.HBM)
        smem = pl.BlockSpec(memory_space=pltpu.SMEM)
        vmem = pl.BlockSpec(memory_space=pltpu.VMEM)
        x, logs = pl.pallas_call(
            functools.partial(kernel, n_vec, n_wlk, vecs, pieces, paired),
            out_shape=(pltpu.VMEM((occ, basis), f32), pltpu.VMEM((8, 128), f32)),
            in_specs=[hbm, hbm, smem, smem, hbm],
            out_specs=(vmem, vmem),
            scratch_shapes=[
                pltpu.VMEM((occ, basis), f32),
                pltpu.VMEM(propagator.shape, f32),
                pltpu.VMEM(propagator.shape, bf16),
                pltpu.VMEM((n_wlk, occ + EXTRA, basis), bf16),
                pltpu.VMEM((basis, walkers * occ), bf16),
                pltpu.VMEM((n_vec, vecs * occ, basis), bf16),
                pltpu.VMEM((walkers * occ, basis), f32),
                pltpu.VMEM((occ, basis), bf16),
                pltpu.VMEM((occ, basis), bf16),
                dma((3,)),
                dma((FULL_PIECES + 3, 1) if paired else (others, pieces)), dma(crossing + (pieces,)), dma((others,)), dma(crossing),
                dma((2 * chips + 1,)), dma, dma, dma, dma, dma((FULL_PIECES,)),
                regular((others,)), regular((chips,)), regular,
            ],
            compiler_params=pltpu.CompilerParams(
                collective_id=0, has_side_effects=True, vmem_limit_bytes=60000000),
        )(
            cholesky.reshape(vecs * occ, basis),
            orbitals.reshape(occ, basis),
            log_weights,
            parents,
            propagator,
        )

        def here(array):
            return pltpu.with_memory_space_constraint(array, pltpu.VMEM)

        out, log = pl.pallas_call(
            deliver,
            out_shape=(
                jax.ShapeDtypeStruct((occ, basis), f32),
                jax.ShapeDtypeStruct((1, 128), f32),
            ),
            in_specs=[vmem, vmem],
            out_specs=(hbm, hbm),
            scratch_shapes=[dma((2,))],
        )(here(x), here(logs))
        return out.reshape(orbitals.shape), log[0, :1]

    placed = (
        P(("grp", "vec"), None, None),
        P(("grp", "vec", "wlk"), None, None),
        P(("grp", "vec", "wlk")),
        P(("grp", "vec", "wlk")),
        P("grp", None),
    )
    return jax.shard_map(
        local,
        mesh=mesh,
        in_specs=placed,
        out_specs=(P(("grp", "vec", "wlk"), None, None), P(("grp", "vec", "wlk"))),
        check_vma=False,
    )
```
